32 devices in a mesh: dp: 8 (over z, x), fsdp: 4 (over y, core).
Axes of the slice: x: 2, y: 2, z: 4, core: 2. Of those that a mesh axis runs over, the one named last changes fastest.
Arguments:
- inputs: bfloat16 [32, 160, 960], P(('dp', 'fsdp')), may hold values from -6 to 6
- cotangent: bfloat16 [32, 160, 960], P(('dp', 'fsdp')), may hold values from -6 to 6
- w_query: bfloat16 [960, 960], P('fsdp'), may hold values from -0.19364917 to 0.19364917
- key_weight: bfloat16 [960, 320], P('fsdp'), may hold values from -6.5 to 6.5
- value_weight: bfloat16 [960, 320], P('fsdp'), may hold values from -0.1875 to 0.1875
- w_output: bfloat16 [960, 960], P('fsdp'), may hold values from -1 to 1
- w_gate: bfloat16 [960, 2560], P('fsdp'), may hold values from -0.1875 to 0.1875
- w_up: bfloat16 [960, 2560], P('fsdp'), may hold values from -0.1875 to 0.1875
- w_down: bfloat16 [2560, 960], P('fsdp'), may hold values from -0.125 to 0.125
- attn_gain: bfloat16 [960], P('fsdp'), may hold values from 0.5 to 1.5
- mlp_gain: bfloat16 [960], P('fsdp'), may hold values from 0.5 to 1.5
Outputs:
- outputs: bfloat16 [32, 160, 960], P(('dp', 'fsdp'))
- grad_inputs: float32 [32, 160, 960], P(('dp', 'fsdp'))
- grad_w_query: float32 [960, 960], P('fsdp')
- grad_w_key: float32 [960, 320], P('fsdp')
- grad_w_value: float32 [960, 320], P('fsdp')
- grad_w_output: float32 [960, 960], P('fsdp')
- grad_w_gate: float32 [960, 2560], P('fsdp')
- grad_w_up: float32 [960, 2560], P('fsdp')
- grad_w_down: float32 [2560, 960], P('fsdp')
- grad_attn_gain: float32 [960], P('fsdp')
- grad_mlp_gain: float32 [960], P('fsdp')
The draws below stay inside these ranges and needn't reach their ends.
All inputs are finite; a program needn't handle non-finite values.
Results may differ from the reference program's by a relative error of at most 0.019.
The reference program's roundings to bfloat16 on the way count: a program that leaves them out, or rounds other values in their place, can miss the bound.
Values may be sent and summed in bfloat16 or wider, within the bound.
A program may use at most 128 MiB of HBM per device.

```python
import math
import jax
import jax.numpy as jnp
from jax import lax

QUERY_HEADS = 15
KEY_VALUE_HEADS = 5
HEAD_DIMENSION = 64
MODEL_WIDTH = 960
FF = 2560
LEN = 160
KV = 320
SEQS = 32
TOKENS = 5120


def query_before_rotation(key):
    return jnp.clip(jax.random.normal(jax.random.fold_in(key, 11), (MODEL_WIDTH, QUERY_HEADS * HEAD_DIMENSION), jnp.float32), -6.0, 6.0)


def draw_w_query(key, part):
    return (query_before_rotation(key) * MODEL_WIDTH ** (-0.5)).astype(jnp.bfloat16)


def draw_key_weight(key, part):
    local_portion = jnp.clip(jax.random.normal(jax.random.fold_in(key, 23), (MODEL_WIDTH, KEY_VALUE_HEADS * HEAD_DIMENSION), jnp.float32), -6.0, 6.0) * MODEL_WIDTH ** (-0.5)
    return local_portion.astype(jnp.bfloat16)


def strengthened(array, stream_key, source, target, parts, factor):
    owner, partner = [(jnp.arange(array.shape[axis_at]) // (array.shape[axis_at] // parts)).reshape([-1 if axis == axis_at else 1 for axis in range(array.ndim)]) for axis_at in (source, target)]
    chosen = jax.random.permutation(stream_key, parts)[partner]
    strong = (owner == chosen) | (owner == (partner + parts // 2) % parts)
    return jnp.where(strong, factor * array, array)


def steps_of(own_key, extent, cuts, smallest, high):
    level, own = 1.0, jax.random.fold_in(own_key, 6)
    for axis_at, shards_of in cuts:
        heights = jnp.exp(jax.random.uniform(jax.random.fold_in(own, axis_at), (shards_of,), jnp.float32, smallest / len(cuts), high / len(cuts)))
        level = level * jnp.repeat(heights, extent[axis_at] // shards_of).reshape([-1 if axis == axis_at else 1 for axis in range(len(extent))])
    return level


def centred(stream_key, dims, deviation, most, cuts=(), kind=jnp.bfloat16):
    loudness = steps_of(stream_key, dims, cuts, -0.22, 0.18) if cuts else 1.0
    result = jax.random.normal(stream_key, dims, jnp.float32) * deviation * loudness
    return jnp.minimum(jnp.maximum(result, -most), most).astype(kind)


def gaussian_with(key, shape, deviation, most, cuts, heavy, kind=jnp.bfloat16):
    entries = deviation * jax.random.normal(key, shape, jnp.float32)
    if cuts:
        entries = entries * steps_of(key, shape, cuts, -0.22, 0.18)
    return jnp.clip(strengthened(entries, jax.random.fold_in(key, 3), *heavy), -most, most).astype(kind)


def setup_inputs(seed: int = 0) -> dict:
    splits = jax.random.split(jax.random.key(seed), 12)
    return {
        "inputs": gaussian_with(splits[0], (SEQS, LEN, MODEL_WIDTH), 1.0, 6.0, ((0, 32),), (0, 2, 32, 2.75)),
        "cotangent": centred(splits[1], (SEQS, LEN, MODEL_WIDTH), 1.0, 6.0, ((0, 32),)),
        "w_query": draw_w_query(jax.random.fold_in(splits[11], 71), 0),
        "key_weight": draw_key_weight(jax.random.fold_in(splits[11], 71), 0),
        "value_weight": centred(splits[4], (MODEL_WIDTH, KV), MODEL_WIDTH ** -0.5, 0.1875, ((0, 4),)),
        "w_output": centred(splits[5], (QUERY_HEADS * HEAD_DIMENSION, MODEL_WIDTH), (MODEL_WIDTH // 32) ** -0.5, 1.0, ((0, 4),)),
        "w_gate": centred(splits[6], (MODEL_WIDTH, FF), MODEL_WIDTH ** -0.5, 0.1875, ((0, 4),)),
        "w_up": centred(splits[7], (MODEL_WIDTH, FF), MODEL_WIDTH ** -0.5, 0.1875, ((0, 4),)),
        "w_down": centred(splits[8], (FF, MODEL_WIDTH), FF ** -0.5, 0.125, ((0, 4),)),
        "attn_gain": jnp.clip(1.0 + 0.1 * jax.random.normal(splits[9], (MODEL_WIDTH,), jnp.float32), 0.5, 1.5).astype(jnp.bfloat16),
        "mlp_gain": jnp.clip(1.0 + 0.1 * jax.random.normal(splits[10], (MODEL_WIDTH,), jnp.float32), 0.5, 1.5).astype(jnp.bfloat16),
    }


EPS = 1e-05
ROPE_BASE = 10000.0

def matrix_product(left_matrix, right_matrix):
    return jnp.dot(left_matrix, right_matrix, preferred_element_type=jnp.float32)

def matmul_tn(left_matrix, right_matrix):
    return lax.dot_general(left_matrix, right_matrix, (((0,), (0,)), ((), ())), preferred_element_type=jnp.float32)

def matmul_nt(left_matrix, right_matrix):
    return lax.dot_general(left_matrix, right_matrix, (((1,), (1,)), ((), ())), preferred_element_type=jnp.float32)

def rope_tables(sequence_length, head_size):
    half_size = head_size // 2
    frequency = ROPE_BASE ** (-(jnp.arange(half_size, dtype=jnp.float32) * (2.0 / head_size)))
    angles = jnp.arange(sequence_length, dtype=jnp.float32)[:, None] * frequency[None, :]
    return (jnp.cos(angles), jnp.sin(angles))

def apply_rotary(tensor, cosine_table, sine_lookup, direction):
    half_size = tensor.shape[-1] // 2
    first_half = tensor[..., :half_size]
    second_half = tensor[..., half_size:]
    cos_wide = cosine_table[None, :, None, :]
    sin_wide = sine_lookup[None, :, None, :]
    return jnp.concatenate([first_half * cos_wide - direction * second_half * sin_wide, second_half * cos_wide + direction * first_half * sin_wide], axis=-1)

def norm_forward(values_in, gain_vec):
    inv_rms = lax.rsqrt(lax.optimization_barrier(jnp.mean(values_in * values_in, axis=-1, keepdims=True)) + EPS)
    unit_rows = values_in * inv_rms
    normed = (unit_rows * gain_vec.astype(jnp.float32)).astype(jnp.bfloat16)
    return (unit_rows, inv_rms, normed)

def norm_backward(grad_out, unit_rows, inv_rms, gain_vec):
    grad_gain = lax.optimization_barrier(jnp.sum(grad_out * unit_rows, axis=(0, 1)))
    grad_unit = grad_out * gain_vec.astype(jnp.float32)
    grad_in = inv_rms * (grad_unit - unit_rows * lax.optimization_barrier(jnp.mean(grad_unit * unit_rows, axis=-1, keepdims=True)))
    return (grad_in, grad_gain)

def scores_of(query_rot, key_rot):
    local_sequences, sequence_length, heads_q, head_size = query_rot.shape
    heads_kv = key_rot.shape[2]
    grouped = query_rot.reshape(local_sequences, sequence_length, heads_kv, heads_q // heads_kv, head_size)
    scores = jnp.einsum('sqhgd,skhd->shgqk', grouped.astype(jnp.float32), key_rot.astype(jnp.float32)) * head_size ** (-0.5)
    positions = jnp.arange(sequence_length)
    allowed = positions[:, None] >= positions[None, :]
    return (grouped, jnp.where(allowed, scores, -1e+30))

def attend(query_rot, key_rot, value_low_precision):
    grouped, scores = scores_of(query_rot, key_rot)
    peak_row = lax.optimization_barrier(jnp.max(scores, axis=-1, keepdims=True))
    logsum = peak_row + jnp.log(lax.optimization_barrier(jnp.sum(jnp.exp(scores - peak_row), axis=-1, keepdims=True)))
    probs_bf = jnp.exp(scores - logsum).astype(jnp.bfloat16)
    attn_mixed = jnp.einsum('shgqk,skhd->sqhgd', probs_bf.astype(jnp.float32), value_low_precision.astype(jnp.float32))
    local_sequences, sequence_length = (query_rot.shape[0], query_rot.shape[1])
    return (attn_mixed.reshape(local_sequences, sequence_length, -1).astype(jnp.bfloat16), logsum)

def attend_back(query_rot, key_rot, value_low_precision, logsum, grad_mixed):
    grouped, scores = scores_of(query_rot, key_rot)
    probs = jnp.exp(scores - logsum)
    probs_bf = probs.astype(jnp.bfloat16)
    grad_grouped = grad_mixed.reshape(grouped.shape).astype(jnp.float32)
    value_gradient = jnp.einsum('shgqk,sqhgd->skhd', probs_bf.astype(jnp.float32), grad_grouped)
    grad_probs = jnp.einsum('sqhgd,skhd->shgqk', grad_grouped, value_low_precision.astype(jnp.float32))
    row_dot = lax.optimization_barrier(jnp.sum(probs * grad_probs, axis=-1, keepdims=True))
    grad_scores = (probs * (grad_probs - row_dot) * query_rot.shape[-1] ** (-0.5)).astype(jnp.bfloat16)
    grad_query = jnp.einsum('shgqk,skhd->sqhgd', grad_scores.astype(jnp.float32), key_rot.astype(jnp.float32))
    key_gradient = jnp.einsum('shgqk,sqhgd->skhd', grad_scores.astype(jnp.float32), grouped.astype(jnp.float32))
    return (grad_query.reshape(query_rot.shape), key_gradient, value_gradient)

def forward_pass(inputs, weights):
    w_query, key_weight, value_weight, w_output, w_gate, w_up, w_down, attn_gain, mlp_gain = weights
    local_sequences, sequence_length, width = inputs.shape
    cosine_table, sine_lookup = rope_tables(sequence_length, HEAD_DIMENSION)
    resid_in = inputs.astype(jnp.float32)
    unit_one, inv_one, normed_one = norm_forward(resid_in, attn_gain)
    flattened_first = normed_one.reshape(-1, width)
    query_proj = matrix_product(flattened_first, w_query).reshape(local_sequences, sequence_length, QUERY_HEADS, HEAD_DIMENSION)
    projected_key = matrix_product(flattened_first, key_weight).reshape(local_sequences, sequence_length, KEY_VALUE_HEADS, HEAD_DIMENSION)
    value_low_precision = matrix_product(flattened_first, value_weight).astype(jnp.bfloat16).reshape(local_sequences, sequence_length, KEY_VALUE_HEADS, HEAD_DIMENSION)
    query_rot = apply_rotary(query_proj, cosine_table, sine_lookup, 1.0).astype(jnp.bfloat16)
    key_rot = apply_rotary(projected_key, cosine_table, sine_lookup, 1.0).astype(jnp.bfloat16)
    attn_mixed, logsum = attend(query_rot, key_rot, value_low_precision)
    flat_mixed = attn_mixed.reshape(-1, QUERY_HEADS * HEAD_DIMENSION)
    resid_mid = resid_in + matrix_product(flat_mixed, w_output).reshape(inputs.shape)
    unit_two, inv_two, normed_two = norm_forward(resid_mid, mlp_gain)
    flat_two = normed_two.reshape(-1, width)
    gate_pre = matrix_product(flat_two, w_gate)
    up_proj = matrix_product(flat_two, w_up)
    sigmoid_gate = jax.nn.sigmoid(gate_pre)
    hidden = (gate_pre * sigmoid_gate * up_proj).astype(jnp.bfloat16)
    outputs = (resid_mid + matrix_product(hidden, w_down).reshape(inputs.shape)).astype(jnp.bfloat16)
    saved = (unit_one, inv_one, flattened_first, query_rot, key_rot, value_low_precision, flat_mixed, logsum, unit_two, inv_two, flat_two, gate_pre, up_proj, sigmoid_gate, hidden)
    return (outputs, saved)

def backward_pass(cotangent, weights, saved):
    w_query, key_weight, value_weight, w_output, w_gate, w_up, w_down, attn_gain, mlp_gain = weights
    unit_one, inv_one, flattened_first, query_rot, key_rot, value_low_precision, flat_mixed, logsum, unit_two, inv_two, flat_two, gate_pre, up_proj, sigmoid_gate, hidden = saved
    local_sequences, sequence_length, width = cotangent.shape
    cosine_table, sine_lookup = rope_tables(sequence_length, HEAD_DIMENSION)
    cot_flat = cotangent.reshape(-1, width)
    sum_down = matmul_tn(hidden, cot_flat)
    grad_hidden = matmul_nt(cot_flat, w_down)
    grad_gate_bf = (grad_hidden * up_proj * sigmoid_gate * (1.0 + gate_pre * (1.0 - sigmoid_gate))).astype(jnp.bfloat16)
    grad_up_bf = (grad_hidden * gate_pre * sigmoid_gate).astype(jnp.bfloat16)
    sum_gate = matmul_tn(flat_two, grad_gate_bf)
    sum_up = matmul_tn(flat_two, grad_up_bf)
    grad_normed_two = matmul_nt(grad_gate_bf, w_gate) + matmul_nt(grad_up_bf, w_up)
    grad_norm_two, sum_mlp_gain = norm_backward(grad_normed_two.reshape(cotangent.shape), unit_two, inv_two, mlp_gain)
    grad_resid_mid = cotangent.astype(jnp.float32) + grad_norm_two
    grad_mid_bf = grad_resid_mid.astype(jnp.bfloat16).reshape(-1, width)
    sum_output = matmul_tn(flat_mixed, grad_mid_bf)
    grad_mixed_bf = matmul_nt(grad_mid_bf, w_output).astype(jnp.bfloat16).reshape(local_sequences, sequence_length, QUERY_HEADS, HEAD_DIMENSION)
    grad_query, key_gradient, value_gradient = attend_back(query_rot, key_rot, value_low_precision, logsum, grad_mixed_bf)
    grad_query_bf = apply_rotary(grad_query, cosine_table, sine_lookup, -1.0).astype(jnp.bfloat16).reshape(-1, QUERY_HEADS * HEAD_DIMENSION)
    key_gradient_low = apply_rotary(key_gradient, cosine_table, sine_lookup, -1.0).astype(jnp.bfloat16).reshape(-1, KEY_VALUE_HEADS * HEAD_DIMENSION)
    value_gradient_low = value_gradient.astype(jnp.bfloat16).reshape(-1, KEY_VALUE_HEADS * HEAD_DIMENSION)
    sum_query = matmul_tn(flattened_first, grad_query_bf)
    sum_key = matmul_tn(flattened_first, key_gradient_low)
    sum_value = matmul_tn(flattened_first, value_gradient_low)
    grad_normed_one = matmul_nt(grad_query_bf, w_query) + matmul_nt(key_gradient_low, key_weight) + matmul_nt(value_gradient_low, value_weight)
    grad_norm_one, sum_attn_gain = norm_backward(grad_normed_one.reshape(cotangent.shape), unit_one, inv_one, attn_gain)
    grad_inputs = grad_resid_mid + grad_norm_one
    return (grad_inputs, (sum_query, sum_key, sum_value, sum_output, sum_gate, sum_up, sum_down, sum_attn_gain, sum_mlp_gain))

def reference(inputs, cotangent, w_query, key_weight, value_weight, w_output, w_gate, w_up, w_down, attn_gain, mlp_gain):
    weights = (w_query, key_weight, value_weight, w_output, w_gate, w_up, w_down, attn_gain, mlp_gain)
    block_seqs = math.gcd(SEQS, 16)
    block_count = SEQS // block_seqs
    shaped_in = inputs.reshape(block_count, block_seqs, LEN, MODEL_WIDTH)
    shaped_cot = cotangent.reshape(block_count, block_seqs, LEN, MODEL_WIDTH)

    def step_block(totals, pieces):
        outputs, saved = forward_pass(pieces[0], weights)
        grad_inputs, grad_parts = backward_pass(pieces[1], weights, saved)
        return (tuple((running + grad_part for running, grad_part in zip(totals, grad_parts))), (outputs, grad_inputs))
    start_sums = tuple((jnp.zeros(weight_arr.shape, jnp.float32) for weight_arr in weights))
    totals, (out_blocks, grad_blocks) = lax.scan(step_block, start_sums, (shaped_in, shaped_cot))
    scale = float(TOKENS) ** (-0.5)
    return (out_blocks.reshape(inputs.shape), grad_blocks.reshape(inputs.shape), totals[0] * scale, totals[1] * scale, totals[2] * scale, totals[3] * scale, totals[4] * scale, totals[5] * scale, totals[6] * scale, totals[7] * scale, totals[8] * scale)
```

```python
import functools

import jax
import jax.numpy as jnp
from jax import lax
from jax.experimental import pallas as pl
from jax.experimental.pallas import tpu as pltpu
from jax.sharding import PartitionSpec as P

QUERY_HEADS = 15
KEY_VALUE_HEADS = 5
HEAD_DIMENSION = 64


EPS = 1e-05
ROPE_BASE = 10000.0


def matrix_product(left_matrix, right_matrix):
    return jnp.dot(left_matrix, right_matrix, preferred_element_type=jnp.float32)


def matmul_tn(left_matrix, right_matrix):
    return lax.dot_general(
        left_matrix, right_matrix, (((0,), (0,)), ((), ())), preferred_element_type=jnp.float32
    )


def matmul_nt(left_matrix, right_matrix):
    return lax.dot_general(
        left_matrix, right_matrix, (((1,), (1,)), ((), ())), preferred_element_type=jnp.float32
    )


def rope_tables(sequence_length, head_size):
    half_size = head_size // 2
    frequency = ROPE_BASE ** (-(jnp.arange(half_size, dtype=jnp.float32) * (2.0 / head_size)))
    angles = jnp.arange(sequence_length, dtype=jnp.float32)[:, None] * frequency[None, :]
    return (jnp.cos(angles), jnp.sin(angles))


def apply_rotary(tensor, cosine_table, sine_lookup, direction):
    half_size = tensor.shape[-1] // 2
    first_half = tensor[..., :half_size]
    second_half = tensor[..., half_size:]
    cos_wide = cosine_table[None, :, None, :]
    sin_wide = sine_lookup[None, :, None, :]
    return jnp.concatenate(
        [
            first_half * cos_wide - direction * second_half * sin_wide,
            second_half * cos_wide + direction * first_half * sin_wide,
        ],
        axis=-1,
    )


def norm_forward(values_in, gain_vec):
    inv_rms = lax.rsqrt(jnp.mean(values_in * values_in, axis=-1, keepdims=True) + EPS)
    unit_rows = values_in * inv_rms
    normed = (unit_rows * gain_vec.astype(jnp.float32)).astype(jnp.bfloat16)
    return (unit_rows, inv_rms, normed)


def norm_backward(grad_out, unit_rows, inv_rms, gain_vec):
    grad_gain = jnp.sum(grad_out * unit_rows, axis=(0, 1))
    grad_unit = grad_out * gain_vec.astype(jnp.float32)
    grad_in = inv_rms * (
        grad_unit - unit_rows * jnp.mean(grad_unit * unit_rows, axis=-1, keepdims=True)
    )
    return (grad_in, grad_gain)


def scores_of(query_rot, key_rot):
    local_sequences, sequence_length, heads_q, head_size = query_rot.shape
    heads_kv = key_rot.shape[2]
    grouped = query_rot.reshape(
        local_sequences, sequence_length, heads_kv, heads_q // heads_kv, head_size
    )
    scores = jnp.einsum(
        "sqhgd,skhd->shgqk", grouped, key_rot, preferred_element_type=jnp.float32
    ) * head_size ** (-0.5)
    positions = jnp.arange(sequence_length)
    allowed = positions[:, None] >= positions[None, :]
    return (grouped, jnp.where(allowed, scores, -1e30))


def attend(query_rot, key_rot, value_low_precision):
    grouped, scores = scores_of(query_rot, key_rot)
    peak_row = jnp.max(scores, axis=-1, keepdims=True)
    logsum = peak_row + jnp.log(jnp.sum(jnp.exp(scores - peak_row), axis=-1, keepdims=True))
    probs_bf = jnp.exp(scores - logsum).astype(jnp.bfloat16)
    attn_mixed = jnp.einsum(
        "shgqk,skhd->sqhgd", probs_bf, value_low_precision, preferred_element_type=jnp.float32
    )
    local_sequences, sequence_length = (query_rot.shape[0], query_rot.shape[1])
    return (attn_mixed.reshape(local_sequences, sequence_length, -1).astype(jnp.bfloat16), logsum)


def attend_back(query_rot, key_rot, value_low_precision, logsum, grad_mixed):
    grouped, scores = scores_of(query_rot, key_rot)
    probs = jnp.exp(scores - logsum)
    probs_bf = probs.astype(jnp.bfloat16)
    grad_grouped = grad_mixed.reshape(grouped.shape)
    value_gradient = jnp.einsum(
        "shgqk,sqhgd->skhd", probs_bf, grad_grouped, preferred_element_type=jnp.float32
    )
    grad_probs = jnp.einsum(
        "sqhgd,skhd->shgqk", grad_grouped, value_low_precision, preferred_element_type=jnp.float32
    )
    row_dot = jnp.sum(probs * grad_probs, axis=-1, keepdims=True)
    grad_scores = (probs * (grad_probs - row_dot) * query_rot.shape[-1] ** (-0.5)).astype(
        jnp.bfloat16
    )
    grad_query = jnp.einsum(
        "shgqk,skhd->sqhgd", grad_scores, key_rot, preferred_element_type=jnp.float32
    )
    key_gradient = jnp.einsum(
        "shgqk,sqhgd->skhd", grad_scores, grouped, preferred_element_type=jnp.float32
    )
    return (grad_query.reshape(query_rot.shape), key_gradient, value_gradient)


def forward_pass(inputs, weights):
    w_query, key_weight, value_weight, w_output, w_gate, w_up, w_down, attn_gain, mlp_gain = weights
    local_sequences, sequence_length, width = inputs.shape
    cosine_table, sine_lookup = rope_tables(sequence_length, HEAD_DIMENSION)
    resid_in = inputs.astype(jnp.float32)
    unit_one, inv_one, normed_one = norm_forward(resid_in, attn_gain)
    flattened_first = normed_one.reshape(-1, width)
    query_proj = matrix_product(flattened_first, w_query).reshape(
        local_sequences, sequence_length, QUERY_HEADS, HEAD_DIMENSION
    )
    projected_key = matrix_product(flattened_first, key_weight).reshape(
        local_sequences, sequence_length, KEY_VALUE_HEADS, HEAD_DIMENSION
    )
    value_low_precision = (
        matrix_product(flattened_first, value_weight)
        .astype(jnp.bfloat16)
        .reshape(local_sequences, sequence_length, KEY_VALUE_HEADS, HEAD_DIMENSION)
    )
    query_rot = apply_rotary(query_proj, cosine_table, sine_lookup, 1.0).astype(jnp.bfloat16)
    key_rot = apply_rotary(projected_key, cosine_table, sine_lookup, 1.0).astype(jnp.bfloat16)
    attn_mixed, logsum = attend(query_rot, key_rot, value_low_precision)
    flat_mixed = attn_mixed.reshape(-1, QUERY_HEADS * HEAD_DIMENSION)
    resid_mid = resid_in + matrix_product(flat_mixed, w_output).reshape(inputs.shape)
    unit_two, inv_two, normed_two = norm_forward(resid_mid, mlp_gain)
    flat_two = normed_two.reshape(-1, width)
    gate_pre = matrix_product(flat_two, w_gate)
    up_proj = matrix_product(flat_two, w_up)
    sigmoid_gate = jax.nn.sigmoid(gate_pre)
    hidden = (gate_pre * sigmoid_gate * up_proj).astype(jnp.bfloat16)
    outputs = (resid_mid + matrix_product(hidden, w_down).reshape(inputs.shape)).astype(
        jnp.bfloat16
    )
    saved = (
        unit_one,
        inv_one,
        flattened_first,
        query_rot,
        key_rot,
        value_low_precision,
        flat_mixed,
        logsum,
        unit_two,
        inv_two,
        flat_two,
        gate_pre,
        up_proj,
        sigmoid_gate,
        hidden,
    )
    return (outputs, saved)


def backward_pass(cotangent, weights, saved):
    w_query, key_weight, value_weight, w_output, w_gate, w_up, w_down, attn_gain, mlp_gain = weights
    (
        unit_one,
        inv_one,
        flattened_first,
        query_rot,
        key_rot,
        value_low_precision,
        flat_mixed,
        logsum,
        unit_two,
        inv_two,
        flat_two,
        gate_pre,
        up_proj,
        sigmoid_gate,
        hidden,
    ) = saved
    local_sequences, sequence_length, width = cotangent.shape
    cosine_table, sine_lookup = rope_tables(sequence_length, HEAD_DIMENSION)
    cot_flat = cotangent.reshape(-1, width)
    sum_down = matmul_tn(cot_flat, hidden)
    grad_hidden = matmul_nt(cot_flat, w_down)
    grad_gate_bf = (
        grad_hidden * up_proj * sigmoid_gate * (1.0 + gate_pre * (1.0 - sigmoid_gate))
    ).astype(jnp.bfloat16)
    grad_up_bf = (grad_hidden * gate_pre * sigmoid_gate).astype(jnp.bfloat16)
    sum_gate = matmul_tn(flat_two, grad_gate_bf)
    sum_up = matmul_tn(flat_two, grad_up_bf)
    grad_normed_two = matmul_nt(grad_gate_bf, w_gate) + matmul_nt(grad_up_bf, w_up)
    grad_norm_two, sum_mlp_gain = norm_backward(
        grad_normed_two.reshape(cotangent.shape), unit_two, inv_two, mlp_gain
    )
    grad_resid_mid = cotangent.astype(jnp.float32) + grad_norm_two
    grad_mid_bf = grad_resid_mid.astype(jnp.bfloat16).reshape(-1, width)
    sum_output = matmul_tn(flat_mixed, grad_mid_bf)
    grad_mixed_bf = (
        matmul_nt(grad_mid_bf, w_output)
        .astype(jnp.bfloat16)
        .reshape(local_sequences, sequence_length, QUERY_HEADS, HEAD_DIMENSION)
    )
    grad_query, key_gradient, value_gradient = attend_back(
        query_rot, key_rot, value_low_precision, logsum, grad_mixed_bf
    )
    grad_query_bf = (
        apply_rotary(grad_query, cosine_table, sine_lookup, -1.0)
        .astype(jnp.bfloat16)
        .reshape(-1, QUERY_HEADS * HEAD_DIMENSION)
    )
    key_gradient_low = (
        apply_rotary(key_gradient, cosine_table, sine_lookup, -1.0)
        .astype(jnp.bfloat16)
        .reshape(-1, KEY_VALUE_HEADS * HEAD_DIMENSION)
    )
    value_gradient_low = value_gradient.astype(jnp.bfloat16).reshape(
        -1, KEY_VALUE_HEADS * HEAD_DIMENSION
    )
    sum_query = matmul_tn(flattened_first, grad_query_bf)
    sum_key = matmul_tn(flattened_first, key_gradient_low)
    sum_value = matmul_tn(flattened_first, value_gradient_low)
    grad_normed_one = (
        matmul_nt(grad_query_bf, w_query)
        + matmul_nt(key_gradient_low, key_weight)
        + matmul_nt(value_gradient_low, value_weight)
    )
    grad_norm_one, sum_attn_gain = norm_backward(
        grad_normed_one.reshape(cotangent.shape), unit_one, inv_one, attn_gain
    )
    grad_inputs = grad_resid_mid + grad_norm_one
    return (
        grad_inputs,
        (
            sum_query,
            sum_key,
            sum_value,
            sum_output,
            sum_gate,
            sum_up,
            sum_down,
            sum_attn_gain,
            sum_mlp_gain,
        ),
    )


CHUNK = 512


def dp_split(n_copies):
    outer = 4 if n_copies % 4 == 0 else 1
    return n_copies // outer, outer


def reduce_kernel(n_copies, n_group, n_blocks, per_block, *refs):
    sources = refs[:n_blocks]
    out_hbm = refs[n_blocks]
    own, from_core, from_pair, from_inner, from_outer, final = refs[n_blocks + 1 : n_blocks + 7]
    (load_sem, store_sem, send_core, recv_core, send_pair, recv_pair, send_in, recv_in,
     send_out, recv_out, send_ago, recv_ago, send_agi, recv_agi) = refs[n_blocks + 7 :]
    inner_n, outer_n = dp_split(n_copies)
    pair_n = n_group // 2
    steps = n_blocks * per_block
    copy_id = lax.axis_index("dp")
    member = lax.axis_index("fsdp")
    pair, core = member // 2, member % 2
    outer, inner = copy_id // inner_n, copy_id % inner_n
    piece = CHUNK // outer_n

    def pair_peer(k):
        return (pair + k) % pair_n

    def inner_peer(k):
        return (inner + k) % inner_n

    def outer_peer(k):
        return (outer + k) % outer_n

    def columns(z):
        return pl.ds(pl.multiple_of(z * piece, piece), piece)

    core_device = (copy_id, pair * 2 + (1 - core))
    barrier = pltpu.get_barrier_semaphore()
    devices = [core_device]
    devices += [(copy_id, pair_peer(k) * 2 + core) for k in range(1, pair_n)]
    devices += [(outer * inner_n + inner_peer(k), member) for k in range(1, inner_n)]
    devices += [(outer_peer(k) * inner_n + inner, member) for k in range(1, outer_n)]
    for device in devices:
        pl.semaphore_signal(
            barrier, inc=1, device_id=device, device_id_type=pl.DeviceIdType.MESH
        )
    pl.semaphore_wait(barrier, len(devices))

    def remote(src, dst, send, recv, device):
        return pltpu.make_async_remote_copy(
            src_ref=src,
            dst_ref=dst,
            send_sem=send,
            recv_sem=recv,
            device_id=device,
            device_id_type=pl.DeviceIdType.MESH,
        )

    def core_copy(t, source, c):
        cols = pl.ds(c * CHUNK, CHUNK)
        return remote(
            source.at[:, 1 - core, :, :, cols],
            from_core.at[t],
            send_core.at[t],
            recv_core.at[t],
            core_device,
        )

    def load_copy(t, source, c):
        cols = pl.ds(c * CHUNK, CHUNK)
        return pltpu.make_async_copy(
            source.at[:, core, :, :, cols], own.at[t], load_sem.at[t]
        )

    def pair_copy(t, k):
        return remote(
            own.at[t, pair_peer(k)],
            from_pair.at[t, k - 1],
            send_pair.at[t, k - 1],
            recv_pair.at[t, k - 1],
            (copy_id, pair_peer(k) * 2 + core),
        )

    def inner_copy(t, k):
        return remote(
            own.at[t, pair, inner_peer(k)],
            from_inner.at[t, k - 1],
            send_in.at[t, k - 1],
            recv_in.at[t, k - 1],
            (outer * inner_n + inner_peer(k), member),
        )

    def outer_copy(t, k):
        return remote(
            own.at[t, pair, inner, :, columns(outer_peer(k))],
            from_outer.at[t, k - 1],
            send_out.at[t, k - 1],
            recv_out.at[t, k - 1],
            (outer_peer(k) * inner_n + inner, member),
        )

    def spread_outer(t, k):
        place = final.at[t, inner, :, columns(outer)]
        return remote(
            place,
            place,
            send_ago.at[t, k - 1],
            recv_ago.at[t, k - 1],
            (outer_peer(k) * inner_n + inner, member),
        )

    def landed_outer(t, k):
        place = final.at[t, inner, :, columns((outer + outer_n - k) % outer_n)]
        return remote(
            place,
            place,
            send_ago.at[t, k - 1],
            recv_ago.at[t, k - 1],
            (outer_peer(k) * inner_n + inner, member),
        )

    def spread_inner(t, k):
        place = final.at[t, inner]
        return remote(
            place,
            place,
            send_agi.at[t, k - 1],
            recv_agi.at[t, k - 1],
            (outer * inner_n + inner_peer(k), member),
        )

    def landed_inner(t, k):
        place = final.at[t, (inner + inner_n - k) % inner_n]
        return remote(
            place,
            place,
            send_agi.at[t, k - 1],
            recv_agi.at[t, k - 1],
            (outer * inner_n + inner_peer(k), member),
        )

    def store_copy(t):
        return pltpu.make_async_copy(final.at[t], out_hbm.at[t], store_sem.at[t])

    for t in range(steps):
        core_copy(t, sources[t // per_block], t % per_block).start()
        load_copy(t, sources[t // per_block], t % per_block).start()

    def stage_core(t):
        core_copy(t, sources[0], 0).wait_recv()
        load_copy(t, sources[0], 0).wait()

        def add(i, carry):
            p, x = i // inner_n, i % inner_n
            total = own[t, p, x].astype(jnp.float32) + from_core[t, p, x].astype(jnp.float32)
            own[t, p, x] = total.astype(own.dtype)
            return carry

        lax.fori_loop(0, pair_n * inner_n, add, 0)
        for k in range(1, pair_n):
            pair_copy(t, k).start()

    def stage_pair(t):
        for k in range(1, pair_n):
            pair_copy(t, k).wait_recv()

        def add(x, carry):
            total = own[t, pair, x].astype(jnp.float32)
            for k in range(1, pair_n):
                total += from_pair[t, k - 1, x].astype(jnp.float32)
            own[t, pair, x] = total.astype(own.dtype)
            return carry

        lax.fori_loop(0, inner_n, add, 0)
        for k in range(1, inner_n):
            inner_copy(t, k).start()

    def stage_inner(t):
        total = own[t, pair, inner].astype(jnp.float32)
        for k in range(1, inner_n):
            inner_copy(t, k).wait_recv()
            total += from_inner[t, k - 1].astype(jnp.float32)
        own[t, pair, inner] = total.astype(own.dtype)
        for k in range(1, outer_n):
            outer_copy(t, k).start()

    def stage_outer(t):
        total = own[t, pair, inner, :, columns(outer)].astype(jnp.float32)
        for k in range(1, outer_n):
            outer_copy(t, k).wait_recv()
            total += from_outer[t, k - 1].astype(jnp.float32)
        final[t, inner, :, columns(outer)] = total.astype(final.dtype)
        for k in range(1, outer_n):
            spread_outer(t, k).start()

    def stage_spread(t):
        for k in range(1, outer_n):
            landed_outer(t, k).wait_recv()
        for k in range(1, inner_n):
            spread_inner(t, k).start()

    def stage_store(t):
        for k in range(1, inner_n):
            landed_inner(t, k).wait_recv()
        store_copy(t).start()

    lags = ((stage_core, 0), (stage_pair, 4), (stage_inner, 6), (stage_outer, 8),
            (stage_spread, 10), (stage_store, 12))

    def step(s, carry):
        for stage, lag in lags:
            @pl.when((s >= lag) & (s < steps + lag))
            def _():
                stage(s - lag)
        return carry

    lax.fori_loop(0, steps + 12, step, 0)

    def drain(t, carry):
        core_copy(t, sources[0], 0).wait_send()
        for k in range(1, pair_n):
            pair_copy(t, k).wait_send()
        for k in range(1, inner_n):
            inner_copy(t, k).wait_send()
            spread_inner(t, k).wait_send()
        for k in range(1, outer_n):
            outer_copy(t, k).wait_send()
            spread_outer(t, k).wait_send()
        store_copy(t).wait()
        return carry

    lax.fori_loop(0, steps, drain, 0)


def reduce_blocks(blocks, n_copies, n_group):
    n_blocks = len(blocks)
    total_rows, total_columns = blocks[0].shape
    inner_n, outer_n = dp_split(n_copies)
    pair_n = n_group // 2
    part = total_rows // (n_group * inner_n)
    per_block = total_columns // CHUNK
    steps = n_blocks * per_block
    piece = CHUNK // outer_n
    bf = jnp.bfloat16
    dma = pltpu.SemaphoreType.DMA

    def many(n):
        return dma((steps, max(n - 1, 1)))

    gathered = pl.pallas_call(
        functools.partial(reduce_kernel, n_copies, n_group, n_blocks, per_block),
        out_shape=jax.ShapeDtypeStruct((steps, inner_n, part, CHUNK), bf),
        in_specs=[pl.BlockSpec(memory_space=pl.ANY)] * n_blocks,
        out_specs=pl.BlockSpec(memory_space=pl.ANY),
        scratch_shapes=[
            pltpu.VMEM((steps, pair_n, inner_n, part, CHUNK), bf),
            pltpu.VMEM((steps, pair_n, inner_n, part, CHUNK), bf),
            pltpu.VMEM((steps, max(pair_n - 1, 1), inner_n, part, CHUNK), bf),
            pltpu.VMEM((steps, max(inner_n - 1, 1), part, CHUNK), bf),
            pltpu.VMEM((steps, max(outer_n - 1, 1), part, piece), bf),
            pltpu.VMEM((steps, inner_n, part, CHUNK), bf),
            dma((steps,)),
            dma((steps,)),
            dma((steps,)),
            dma((steps,)),
            many(pair_n),
            many(pair_n),
            many(inner_n),
            many(inner_n),
            many(outer_n),
            many(outer_n),
            many(outer_n),
            many(outer_n),
            many(inner_n),
            many(inner_n),
        ],
        compiler_params=pltpu.CompilerParams(
            collective_id=0, has_side_effects=True, vmem_limit_bytes=60 * 1024 * 1024
        ),
    )(*(b.reshape(pair_n, 2, inner_n, part, total_columns) for b in blocks))
    gathered = gathered.reshape(n_blocks, per_block, inner_n * part, CHUNK)
    return [
        gathered[b].transpose(1, 0, 2).reshape(inner_n * part, total_columns)
        for b in range(n_blocks)
    ]


def per_device(
    inputs,
    cotangent,
    w_query,
    key_weight,
    value_weight,
    w_output,
    w_gate,
    w_up,
    w_down,
    attn_gain,
    mlp_gain,
):
    gathered = (
        lax.all_gather(w_query, "fsdp", axis=0, tiled=True),
        lax.all_gather(key_weight, "fsdp", axis=0, tiled=True),
        lax.all_gather(value_weight, "fsdp", axis=0, tiled=True),
        lax.all_gather(w_output, "fsdp", axis=0, tiled=True),
        lax.all_gather(w_gate, "fsdp", axis=0, tiled=True),
        lax.all_gather(w_up, "fsdp", axis=0, tiled=True),
        lax.all_gather(w_down, "fsdp", axis=0, tiled=True),
        lax.all_gather(attn_gain, "fsdp", axis=0, tiled=True),
        lax.all_gather(mlp_gain, "fsdp", axis=0, tiled=True),
    )
    outputs, saved = forward_pass(inputs, gathered)
    grad_inputs, grads = backward_pass(cotangent, gathered, saved)
    n_copies = lax.axis_size("dp")
    n_group = lax.axis_size("fsdp")
    scale = float(n_copies * n_group * inputs.shape[0] * inputs.shape[1]) ** (-0.5)
    width = inputs.shape[-1]
    rows = width // n_group
    ff_part = w_down.shape[0]
    bf = jnp.bfloat16
    attn_block = jnp.concatenate([g.astype(bf) for g in grads[:4]], axis=1)
    down_block = (
        grads[6]
        .astype(bf)
        .reshape(n_group, rows, n_group, ff_part)
        .transpose(2, 1, 0, 3)
        .reshape(width, n_group * ff_part)
    )
    blocks = (attn_block, grads[4].astype(bf), grads[5].astype(bf), down_block)
    totals = reduce_blocks(blocks, n_copies, n_group)
    total_attn, total_gate, total_up, total_down = [
        t.astype(jnp.float32) * scale for t in totals
    ]
    cut = [w_query.shape[1], key_weight.shape[1], value_weight.shape[1], w_output.shape[1]]
    edges = [sum(cut[:k]) for k in range(5)]
    total_down = (
        total_down.reshape(rows, n_group, ff_part).transpose(2, 1, 0).reshape(ff_part, n_group, rows)
    )
    gain_totals = lax.psum(jnp.stack([grads[7], grads[8]]), ("dp", "fsdp"))
    gain_shard = scale * lax.dynamic_slice_in_dim(
        gain_totals, lax.axis_index("fsdp") * rows, rows, axis=1
    )
    return (
        outputs,
        grad_inputs,
        *(total_attn[:, edges[k] : edges[k + 1]] for k in range(4)),
        total_gate,
        total_up,
        total_down.reshape(ff_part, width),
        gain_shard[0],
        gain_shard[1],
    )


def solution(mesh):
    return jax.shard_map(
        per_device,
        mesh=mesh,
        in_specs=(
            P(("dp", "fsdp"), None, None),
            P(("dp", "fsdp"), None, None),
            P("fsdp", None),
            P("fsdp", None),
            P("fsdp", None),
            P("fsdp", None),
            P("fsdp", None),
            P("fsdp", None),
            P("fsdp", None),
            P("fsdp"),
            P("fsdp"),
        ),
        out_specs=(
            P(("dp", "fsdp"), None, None),
            P(("dp", "fsdp"), None, None),
            P("fsdp", None),
            P("fsdp", None),
            P("fsdp", None),
            P("fsdp", None),
            P("fsdp", None),
            P("fsdp", None),
            P("fsdp", None),
            P("fsdp"),
            P("fsdp"),
        ),
        check_vma=False,
    )
```

```python
import functools

import jax
import jax.numpy as jnp
from jax import lax
from jax.experimental import pallas as pl
from jax.experimental.pallas import tpu as pltpu
from jax.sharding import PartitionSpec as P

QUERY_HEADS = 15
KEY_VALUE_HEADS = 5
HEAD_DIMENSION = 64


EPS = 1e-05
ROPE_BASE = 10000.0


def matrix_product(left_matrix, right_matrix):
    return jnp.dot(left_matrix, right_matrix, preferred_element_type=jnp.float32)


def matmul_tn(left_matrix, right_matrix):
    return lax.dot_general(
        left_matrix, right_matrix, (((0,), (0,)), ((), ())), preferred_element_type=jnp.float32
    )


def matmul_nt(left_matrix, right_matrix):
    return lax.dot_general(
        left_matrix, right_matrix, (((1,), (1,)), ((), ())), preferred_element_type=jnp.float32
    )


def rope_tables(sequence_length, head_size):
    half_size = head_size // 2
    frequency = ROPE_BASE ** (-(jnp.arange(half_size, dtype=jnp.float32) * (2.0 / head_size)))
    angles = jnp.arange(sequence_length, dtype=jnp.float32)[:, None] * frequency[None, :]
    return (jnp.cos(angles), jnp.sin(angles))


def apply_rotary(tensor, cosine_table, sine_lookup, direction):
    half_size = tensor.shape[-1] // 2
    first_half = tensor[..., :half_size]
    second_half = tensor[..., half_size:]
    cos_wide = cosine_table[None, :, None, :]
    sin_wide = sine_lookup[None, :, None, :]
    return jnp.concatenate(
        [
            first_half * cos_wide - direction * second_half * sin_wide,
            second_half * cos_wide + direction * first_half * sin_wide,
        ],
        axis=-1,
    )


def norm_forward(values_in, gain_vec):
    inv_rms = lax.rsqrt(jnp.mean(values_in * values_in, axis=-1, keepdims=True) + EPS)
    unit_rows = values_in * inv_rms
    normed = (unit_rows * gain_vec.astype(jnp.float32)).astype(jnp.bfloat16)
    return (unit_rows, inv_rms, normed)


def norm_backward(grad_out, unit_rows, inv_rms, gain_vec):
    grad_gain = jnp.sum(grad_out * unit_rows, axis=(0, 1))
    grad_unit = grad_out * gain_vec.astype(jnp.float32)
    grad_in = inv_rms * (
        grad_unit - unit_rows * jnp.mean(grad_unit * unit_rows, axis=-1, keepdims=True)
    )
    return (grad_in, grad_gain)


def scores_of(query_rot, key_rot):
    local_sequences, sequence_length, heads_q, head_size = query_rot.shape
    heads_kv = key_rot.shape[2]
    grouped = query_rot.reshape(
        local_sequences, sequence_length, heads_kv, heads_q // heads_kv, head_size
    )
    scores = jnp.einsum(
        "sqhgd,skhd->shgqk", grouped, key_rot, preferred_element_type=jnp.float32
    ) * head_size ** (-0.5)
    positions = jnp.arange(sequence_length)
    allowed = positions[:, None] >= positions[None, :]
    return (grouped, jnp.where(allowed, scores, -1e30))


def attend(query_rot, key_rot, value_low_precision):
    grouped, scores = scores_of(query_rot, key_rot)
    peak_row = jnp.max(scores, axis=-1, keepdims=True)
    logsum = peak_row + jnp.log(jnp.sum(jnp.exp(scores - peak_row), axis=-1, keepdims=True))
    probs_bf = jnp.exp(scores - logsum).astype(jnp.bfloat16)
    attn_mixed = jnp.einsum(
        "shgqk,skhd->sqhgd", probs_bf, value_low_precision, preferred_element_type=jnp.float32
    )
    local_sequences, sequence_length = (query_rot.shape[0], query_rot.shape[1])
    return (attn_mixed.reshape(local_sequences, sequence_length, -1).astype(jnp.bfloat16), logsum)


def attend_back(query_rot, key_rot, value_low_precision, logsum, grad_mixed):
    grouped, scores = scores_of(query_rot, key_rot)
    probs = jnp.exp(scores - logsum)
    probs_bf = probs.astype(jnp.bfloat16)
    grad_grouped = grad_mixed.reshape(grouped.shape)
    value_gradient = jnp.einsum(
        "shgqk,sqhgd->skhd", probs_bf, grad_grouped, preferred_element_type=jnp.float32
    )
    grad_probs = jnp.einsum(
        "sqhgd,skhd->shgqk", grad_grouped, value_low_precision, preferred_element_type=jnp.float32
    )
    row_dot = jnp.sum(probs * grad_probs, axis=-1, keepdims=True)
    grad_scores = (probs * (grad_probs - row_dot) * query_rot.shape[-1] ** (-0.5)).astype(
        jnp.bfloat16
    )
    grad_query = jnp.einsum(
        "shgqk,skhd->sqhgd", grad_scores, key_rot, preferred_element_type=jnp.float32
    )
    key_gradient = jnp.einsum(
        "shgqk,sqhgd->skhd", grad_scores, grouped, preferred_element_type=jnp.float32
    )
    return (grad_query.reshape(query_rot.shape), key_gradient, value_gradient)


def forward_pass(inputs, weights):
    w_query, key_weight, value_weight, w_output, w_gate, w_up, w_down, attn_gain, mlp_gain = weights
    local_sequences, sequence_length, width = inputs.shape
    cosine_table, sine_lookup = rope_tables(sequence_length, HEAD_DIMENSION)
    resid_in = inputs.astype(jnp.float32)
    unit_one, inv_one, normed_one = norm_forward(resid_in, attn_gain)
    flattened_first = normed_one.reshape(-1, width)
    query_proj = matrix_product(flattened_first, w_query).reshape(
        local_sequences, sequence_length, QUERY_HEADS, HEAD_DIMENSION
    )
    projected_key = matrix_product(flattened_first, key_weight).reshape(
        local_sequences, sequence_length, KEY_VALUE_HEADS, HEAD_DIMENSION
    )
    value_low_precision = (
        matrix_product(flattened_first, value_weight)
        .astype(jnp.bfloat16)
        .reshape(local_sequences, sequence_length, KEY_VALUE_HEADS, HEAD_DIMENSION)
    )
    query_rot = apply_rotary(query_proj, cosine_table, sine_lookup, 1.0).astype(jnp.bfloat16)
    key_rot = apply_rotary(projected_key, cosine_table, sine_lookup, 1.0).astype(jnp.bfloat16)
    attn_mixed, logsum = attend(query_rot, key_rot, value_low_precision)
    flat_mixed = attn_mixed.reshape(-1, QUERY_HEADS * HEAD_DIMENSION)
    resid_mid = resid_in + matrix_product(flat_mixed, w_output).reshape(inputs.shape)
    unit_two, inv_two, normed_two = norm_forward(resid_mid, mlp_gain)
    flat_two = normed_two.reshape(-1, width)
    gate_pre = matrix_product(flat_two, w_gate)
    up_proj = matrix_product(flat_two, w_up)
    sigmoid_gate = jax.nn.sigmoid(gate_pre)
    hidden = (gate_pre * sigmoid_gate * up_proj).astype(jnp.bfloat16)
    outputs = (resid_mid + matrix_product(hidden, w_down).reshape(inputs.shape)).astype(
        jnp.bfloat16
    )
    saved = (
        unit_one,
        inv_one,
        flattened_first,
        query_rot,
        key_rot,
        value_low_precision,
        flat_mixed,
        logsum,
        unit_two,
        inv_two,
        flat_two,
        gate_pre,
        up_proj,
        sigmoid_gate,
        hidden,
    )
    return (outputs, saved)


def backward_pass(cotangent, weights, saved):
    w_query, key_weight, value_weight, w_output, w_gate, w_up, w_down, attn_gain, mlp_gain = weights
    (
        unit_one,
        inv_one,
        flattened_first,
        query_rot,
        key_rot,
        value_low_precision,
        flat_mixed,
        logsum,
        unit_two,
        inv_two,
        flat_two,
        gate_pre,
        up_proj,
        sigmoid_gate,
        hidden,
    ) = saved
    local_sequences, sequence_length, width = cotangent.shape
    cosine_table, sine_lookup = rope_tables(sequence_length, HEAD_DIMENSION)
    cot_flat = cotangent.reshape(-1, width)
    sum_down = matmul_tn(cot_flat, hidden)
    grad_hidden = matmul_nt(cot_flat, w_down)
    grad_gate_bf = (
        grad_hidden * up_proj * sigmoid_gate * (1.0 + gate_pre * (1.0 - sigmoid_gate))
    ).astype(jnp.bfloat16)
    grad_up_bf = (grad_hidden * gate_pre * sigmoid_gate).astype(jnp.bfloat16)
    sum_gate = matmul_tn(flat_two, grad_gate_bf)
    sum_up = matmul_tn(flat_two, grad_up_bf)
    grad_normed_two = matmul_nt(grad_gate_bf, w_gate) + matmul_nt(grad_up_bf, w_up)
    grad_norm_two, sum_mlp_gain = norm_backward(
        grad_normed_two.reshape(cotangent.shape), unit_two, inv_two, mlp_gain
    )
    grad_resid_mid = cotangent.astype(jnp.float32) + grad_norm_two
    grad_mid_bf = grad_resid_mid.astype(jnp.bfloat16).reshape(-1, width)
    sum_output = matmul_tn(flat_mixed, grad_mid_bf)
    grad_mixed_bf = (
        matmul_nt(grad_mid_bf, w_output)
        .astype(jnp.bfloat16)
        .reshape(local_sequences, sequence_length, QUERY_HEADS, HEAD_DIMENSION)
    )
    grad_query, key_gradient, value_gradient = attend_back(
        query_rot, key_rot, value_low_precision, logsum, grad_mixed_bf
    )
    grad_query_bf = (
        apply_rotary(grad_query, cosine_table, sine_lookup, -1.0)
        .astype(jnp.bfloat16)
        .reshape(-1, QUERY_HEADS * HEAD_DIMENSION)
    )
    key_gradient_low = (
        apply_rotary(key_gradient, cosine_table, sine_lookup, -1.0)
        .astype(jnp.bfloat16)
        .reshape(-1, KEY_VALUE_HEADS * HEAD_DIMENSION)
    )
    value_gradient_low = value_gradient.astype(jnp.bfloat16).reshape(
        -1, KEY_VALUE_HEADS * HEAD_DIMENSION
    )
    sum_query = matmul_tn(flattened_first, grad_query_bf)
    sum_key = matmul_tn(flattened_first, key_gradient_low)
    sum_value = matmul_tn(flattened_first, value_gradient_low)
    grad_normed_one = (
        matmul_nt(grad_query_bf, w_query)
        + matmul_nt(key_gradient_low, key_weight)
        + matmul_nt(value_gradient_low, value_weight)
    )
    grad_norm_one, sum_attn_gain = norm_backward(
        grad_normed_one.reshape(cotangent.shape), unit_one, inv_one, attn_gain
    )
    grad_inputs = grad_resid_mid + grad_norm_one
    return (
        grad_inputs,
        (
            sum_query,
            sum_key,
            sum_value,
            sum_output,
            sum_gate,
            sum_up,
            sum_down,
            sum_attn_gain,
            sum_mlp_gain,
        ),
    )


CHUNK = 512


def dp_split(n_copies):
    outer = 4 if n_copies % 4 == 0 else 1
    return n_copies // outer, outer


def reduce_kernel(n_copies, n_group, per_block, down_direct, *refs):
    sources = refs[:5]
    out_hbm, out_down, out_gain = refs[5:8]
    own, from_core, from_pair, from_inner, from_outer, final = refs[8:14]
    (load_sem, store_sem, send_core, recv_core, send_pair, recv_pair, send_in, recv_in,
     send_out, recv_out, send_ago, recv_ago, send_agi, recv_agi) = refs[14:]
    inner_n, outer_n = dp_split(n_copies)
    pair_n = n_group // 2
    steps = 4 * per_block + 1
    down_start = 3 * per_block
    copy_id = lax.axis_index("dp")
    member = lax.axis_index("fsdp")
    pair, core = member // 2, member % 2
    outer, inner = copy_id // inner_n, copy_id % inner_n
    piece = CHUNK // outer_n

    def pair_peer(k):
        return (pair + k) % pair_n

    def inner_peer(k):
        return (inner + k) % inner_n

    def outer_peer(k):
        return (outer + k) % outer_n

    def columns(z):
        return pl.ds(pl.multiple_of(z * piece, piece), piece)

    core_device = (copy_id, pair * 2 + (1 - core))
    barrier = pltpu.get_barrier_semaphore()
    devices = [core_device]
    devices += [(copy_id, pair_peer(k) * 2 + core) for k in range(1, pair_n)]
    devices += [(outer * inner_n + inner_peer(k), member) for k in range(1, inner_n)]
    devices += [(outer_peer(k) * inner_n + inner, member) for k in range(1, outer_n)]
    for device in devices:
        pl.semaphore_signal(
            barrier, inc=1, device_id=device, device_id_type=pl.DeviceIdType.MESH
        )
    pl.semaphore_wait(barrier, len(devices))

    def remote(src, dst, send, recv, device):
        return pltpu.make_async_remote_copy(
            src_ref=src,
            dst_ref=dst,
            send_sem=send,
            recv_sem=recv,
            device_id=device,
            device_id_type=pl.DeviceIdType.MESH,
        )

    def core_copy(t, source, c):
        cols = pl.ds(c * CHUNK, CHUNK)
        return remote(
            source.at[:, 1 - core, :, :, cols],
            from_core.at[t],
            send_core.at[t],
            recv_core.at[t],
            core_device,
        )

    def load_copy(t, source, c):
        cols = pl.ds(c * CHUNK, CHUNK)
        return pltpu.make_async_copy(
            source.at[:, core, :, :, cols], own.at[t], load_sem.at[t]
        )

    def pair_copy(t, k):
        return remote(
            own.at[t, pair_peer(k)],
            from_pair.at[t, k - 1],
            send_pair.at[t, k - 1],
            recv_pair.at[t, k - 1],
            (copy_id, pair_peer(k) * 2 + core),
        )

    def inner_copy(t, k):
        return remote(
            own.at[t, pair, inner_peer(k)],
            from_inner.at[t, k - 1],
            send_in.at[t, k - 1],
            recv_in.at[t, k - 1],
            (outer * inner_n + inner_peer(k), member),
        )

    def outer_copy(t, k):
        return remote(
            own.at[t, pair, inner, :, columns(outer_peer(k))],
            from_outer.at[t, k - 1],
            send_out.at[t, k - 1],
            recv_out.at[t, k - 1],
            (outer_peer(k) * inner_n + inner, member),
        )

    def spread_outer(t, k):
        place = final.at[t, inner, :, columns(outer)]
        return remote(
            place,
            place,
            send_ago.at[t, k - 1],
            recv_ago.at[t, k - 1],
            (outer_peer(k) * inner_n + inner, member),
        )

    def landed_outer(t, k):
        place = final.at[t, inner, :, columns((outer + outer_n - k) % outer_n)]
        return remote(
            place,
            place,
            send_ago.at[t, k - 1],
            recv_ago.at[t, k - 1],
            (outer_peer(k) * inner_n + inner, member),
        )

    def spread_inner(t, k):
        place = final.at[t, inner]
        return remote(
            place,
            place,
            send_agi.at[t, k - 1],
            recv_agi.at[t, k - 1],
            (outer * inner_n + inner_peer(k), member),
        )

    def landed_inner(t, k):
        place = final.at[t, (inner + inner_n - k) % inner_n]
        return remote(
            place,
            place,
            send_agi.at[t, k - 1],
            recv_agi.at[t, k - 1],
            (outer * inner_n + inner_peer(k), member),
        )

    def store_copy(t, target):
        return pltpu.make_async_copy(final.at[t], target, store_sem.at[t])

    def start_store(t):
        @pl.when(t < down_start)
        def _():
            cols = pl.ds(pl.multiple_of(lax.rem(t, per_block) * CHUNK, CHUNK), CHUNK)
            store_copy(t, out_hbm.at[t // per_block, :, :, cols]).start()

        @pl.when((t >= down_start) & (t < steps - 1))
        def _():
            c = t - down_start
            if down_direct:
                cols = pl.ds(pl.multiple_of(c * tile, tile), tile)
                for b in range(n_group):
                    pltpu.make_async_copy(
                        final.at[t, :, :, pl.ds(b * tile, tile)],
                        out_down.at[b, :, :, cols],
                        store_sem.at[t],
                    ).start()
            else:
                cols = pl.ds(pl.multiple_of(c * CHUNK, CHUNK), CHUNK)
                store_copy(t, out_down.at[:, :, cols]).start()

        @pl.when(t == steps - 1)
        def _():
            store_copy(t, out_gain).start()

    tile = CHUNK // n_group
    part_width = sources[3].shape[-1] // n_group
    for t in range(steps):
        block, c = t // per_block, t % per_block
        if block == 3 and down_direct:
            for p in range(pair_n):
                for b in range(n_group):
                    place = (slice(None), slice(None), pl.ds(b * tile, tile))
                    theirs = pl.multiple_of((p * 2 + 1 - core) * part_width + c * tile, tile)
                    mine = pl.multiple_of((p * 2 + core) * part_width + c * tile, tile)
                    remote(
                        sources[3].at[b, :, :, pl.ds(theirs, tile)],
                        from_core.at[(t, p) + place],
                        send_core.at[t],
                        recv_core.at[t],
                        core_device,
                    ).start()
                    pltpu.make_async_copy(
                        sources[3].at[b, :, :, pl.ds(mine, tile)],
                        own.at[(t, p) + place],
                        load_sem.at[t],
                    ).start()
        else:
            core_copy(t, sources[block], c).start()
            load_copy(t, sources[block], c).start()

    def stage_core(t):
        core_copy(t, sources[0], 0).wait_recv()
        load_copy(t, sources[0], 0).wait()

        def add(i, carry):
            p, x = i // inner_n, i % inner_n
            total = own[t, p, x].astype(jnp.float32) + from_core[t, p, x].astype(jnp.float32)
            own[t, p, x] = total.astype(own.dtype)
            return carry

        lax.fori_loop(0, pair_n * inner_n, add, 0)
        for k in range(1, pair_n):
            pair_copy(t, k).start()

    def stage_pair(t):
        for k in range(1, pair_n):
            pair_copy(t, k).wait_recv()

        def add(x, carry):
            total = own[t, pair, x].astype(jnp.float32)
            for k in range(1, pair_n):
                total += from_pair[t, k - 1, x].astype(jnp.float32)
            own[t, pair, x] = total.astype(own.dtype)
            return carry

        lax.fori_loop(0, inner_n, add, 0)
        for k in range(1, inner_n):
            inner_copy(t, k).start()

    def stage_inner(t):
        total = own[t, pair, inner].astype(jnp.float32)
        for k in range(1, inner_n):
            inner_copy(t, k).wait_recv()
            total += from_inner[t, k - 1].astype(jnp.float32)
        own[t, pair, inner] = total.astype(own.dtype)
        for k in range(1, outer_n):
            outer_copy(t, k).start()

    def stage_outer(t):
        total = own[t, pair, inner, :, columns(outer)].astype(jnp.float32)
        for k in range(1, outer_n):
            outer_copy(t, k).wait_recv()
            total += from_outer[t, k - 1].astype(jnp.float32)
        final[t, inner, :, columns(outer)] = total.astype(final.dtype)
        for k in range(1, outer_n):
            spread_outer(t, k).start()

    def stage_spread(t):
        for k in range(1, outer_n):
            landed_outer(t, k).wait_recv()
        for k in range(1, inner_n):
            spread_inner(t, k).start()

    def stage_store(t):
        for k in range(1, inner_n):
            landed_inner(t, k).wait_recv()
        start_store(t)

    lags = ((stage_core, 0), (stage_pair, 4), (stage_inner, 6), (stage_outer, 8),
            (stage_spread, 10), (stage_store, 12))

    def step(s, carry):
        for stage, lag in lags:
            @pl.when((s >= lag) & (s < steps + lag))
            def _():
                stage(s - lag)
        return carry

    lax.fori_loop(0, steps + 12, step, 0)

    def drain(t, carry):
        core_copy(t, sources[0], 0).wait_send()
        for k in range(1, pair_n):
            pair_copy(t, k).wait_send()
        for k in range(1, inner_n):
            inner_copy(t, k).wait_send()
            spread_inner(t, k).wait_send()
        for k in range(1, outer_n):
            outer_copy(t, k).wait_send()
            spread_outer(t, k).wait_send()
        store_copy(t, out_gain).wait()
        return carry

    lax.fori_loop(0, steps, drain, 0)


def reduce_blocks(blocks, down, gains, n_copies, n_group):
    total_rows, total_columns = blocks[0].shape
    inner_n, outer_n = dp_split(n_copies)
    pair_n = n_group // 2
    part = total_rows // (n_group * inner_n)
    per_block = total_columns // CHUNK
    steps = 4 * per_block + 1
    part_width = total_columns // n_group
    down_direct = n_group * 128 == CHUNK and part_width % 128 == 0
    piece = CHUNK // outer_n
    bf = jnp.bfloat16
    dma = pltpu.SemaphoreType.DMA

    def many(n):
        return dma((steps, max(n - 1, 1)))

    grouped = (pair_n, 2, inner_n, part)
    if down_direct:
        down = down.reshape(n_group, inner_n, part, total_columns)
        down_shape = (n_group, inner_n, part, part_width)
    else:
        down = (
            down.reshape(n_group, total_rows // n_group, n_group, part_width)
            .transpose(2, 1, 0, 3)
            .reshape(*grouped, total_columns)
        )
        down_shape = (inner_n, part, total_columns)
    gain_width = gains.shape[-1]
    gains = (
        jnp.pad(gains, ((0, 0), (0, inner_n * part * CHUNK - gain_width)))
        .reshape(*grouped, CHUNK)
    )
    big, down_sum, gain_sum = pl.pallas_call(
        functools.partial(reduce_kernel, n_copies, n_group, per_block, down_direct),
        out_shape=[
            jax.ShapeDtypeStruct((3, inner_n, part, total_columns), bf),
            jax.ShapeDtypeStruct(down_shape, bf),
            jax.ShapeDtypeStruct((inner_n, part, CHUNK), bf),
        ],
        in_specs=[pl.BlockSpec(memory_space=pl.ANY)] * 5,
        out_specs=[pl.BlockSpec(memory_space=pl.ANY)] * 3,
        scratch_shapes=[
            pltpu.VMEM((steps, pair_n, inner_n, part, CHUNK), bf),
            pltpu.VMEM((steps, pair_n, inner_n, part, CHUNK), bf),
            pltpu.VMEM((steps, max(pair_n - 1, 1), inner_n, part, CHUNK), bf),
            pltpu.VMEM((steps, max(inner_n - 1, 1), part, CHUNK), bf),
            pltpu.VMEM((steps, max(outer_n - 1, 1), part, piece), bf),
            pltpu.VMEM((steps, inner_n, part, CHUNK), bf),
            dma((steps,)),
            dma((steps,)),
            dma((steps,)),
            dma((steps,)),
            many(pair_n),
            many(pair_n),
            many(inner_n),
            many(inner_n),
            many(outer_n),
            many(outer_n),
            many(outer_n),
            many(outer_n),
            many(inner_n),
            many(inner_n),
        ],
        compiler_params=pltpu.CompilerParams(
            collective_id=0, has_side_effects=True, vmem_limit_bytes=60 * 1024 * 1024
        ),
    )(*(b.reshape(*grouped, total_columns) for b in blocks), down, gains)
    rows = inner_n * part
    big = big.reshape(3, rows, total_columns)
    if down_direct:
        down_sum = down_sum.reshape(total_rows, part_width)
    else:
        down_sum = (
            down_sum.reshape(rows, n_group, part_width).transpose(1, 0, 2).reshape(total_rows, part_width)
        )
    return big, down_sum, gain_sum.reshape(-1)[:gain_width]


def gather_kernel(n_copies, n_group, *refs):
    shards = refs[:5]
    outs = refs[5:10]
    (own_sem, core_send, core_recv, pair_send, pair_recv, in_send, in_recv, out_send, out_recv,
     diag_send, diag_recv, piece_send, piece_recv, gain_send, gain_recv) = refs[10:]
    inner_n, outer_n = dp_split(n_copies)
    pair_n = n_group // 2
    copy_id = lax.axis_index("dp")
    member = lax.axis_index("fsdp")
    pair, core = member // 2, member % 2
    outer, inner = copy_id // inner_n, copy_id % inner_n
    a_bit, b_bit = inner % 2, outer % 2
    a_device = (outer * inner_n + inner + 1 - 2 * a_bit, member)
    b_device = ((outer + 1 - 2 * b_bit) * inner_n + inner, member)
    core_device = (copy_id, pair * 2 + 1 - core)

    def peer(k):
        return (copy_id, ((pair + k) % pair_n) * 2 + core)

    devices = [core_device, a_device, b_device]
    devices += [peer(k) for k in range(1, pair_n)]
    devices += [(copy_id, ((pair + k) % pair_n) * 2 + 1 - core) for k in range(1, pair_n)]
    barrier = pltpu.get_barrier_semaphore()
    for device in devices:
        pl.semaphore_signal(
            barrier, inc=1, device_id=device, device_id_type=pl.DeviceIdType.MESH
        )
    pl.semaphore_wait(barrier, len(devices))

    def remote(src, dst, send, recv, device):
        return pltpu.make_async_remote_copy(
            src_ref=src,
            dst_ref=dst,
            send_sem=send,
            recv_sem=recv,
            device_id=device,
            device_id_type=pl.DeviceIdType.MESH,
        )

    def cut(ref, w, q):
        rows, columns = shards[w].shape
        if w < 3:
            size = columns // 4
            return ref.at[:, pl.ds(pl.multiple_of(q * size, size), size)]
        size = rows // 4
        return ref.at[pl.ds(pl.multiple_of(q * size, size), size), :]

    def index(a, b):
        return a * 2 + b

    pieces = (
        index(a_bit, b_bit),
        index(1 - a_bit, b_bit),
        index(a_bit, 1 - b_bit),
        index(1 - a_bit, 1 - b_bit),
    )
    route = ("a", "b", "y", "y")
    pending = []

    def launch(copy):
        copy.start()
        pending.append(copy)

    def source(k):
        return ((pair + pair_n - k) % pair_n) * 2 + core

    def arrived(w, k, kind, send, recv):
        place = cut(outs[w].at[source(k)], w, pieces[kind])
        return remote(place, place, send.at[w, k - 1], recv.at[w, k - 1], core_device)

    def pass_on(w, k, kind, send, recv, device):
        place = cut(outs[w].at[source(k)], w, pieces[kind])
        launch(remote(place, place, send.at[w, k - 1], recv.at[w, k - 1], device))

    def to_core(w, k, kind):
        place = cut(outs[w].at[source(k)], w, pieces[kind])
        launch(
            remote(
                place, place, piece_send.at[w, k - 1, kind], piece_recv.at[w, k - 1, kind],
                core_device,
            )
        )

    gain_peers = [core_device]
    gain_peers += [(copy_id, ((pair + k) % pair_n) * 2 + core) for k in range(1, pair_n)]
    gain_peers += [(copy_id, ((pair + k) % pair_n) * 2 + 1 - core) for k in range(1, pair_n)]
    for k, device in enumerate(gain_peers):
        launch(remote(shards[4], outs[4].at[member], gain_send.at[k], gain_recv.at[k], device))
    for w in range(4):
        for k in range(1, pair_n):
            launch(
                remote(
                    cut(shards[w], w, pieces[0]),
                    cut(outs[w].at[member], w, pieces[0]),
                    pair_send.at[w, k - 1],
                    pair_recv.at[w, k - 1],
                    peer(k),
                )
            )
    for w in range(4):
        if route[w] == "y":
            for k in range(1, pair_n):
                launch(
                    remote(
                        cut(shards[w], w, pieces[3]),
                        cut(outs[w].at[member], w, pieces[3]),
                        diag_send.at[w, k - 1],
                        diag_recv.at[w, k - 1],
                        peer(k),
                    )
                )
    locals_ = []
    for w in range(4):
        launch(remote(shards[w], outs[w].at[member], core_send.at[w], core_recv.at[w], core_device))
    for w in range(5):
        copy = pltpu.make_async_copy(shards[w], outs[w].at[member], own_sem.at[w])
        copy.start()
        locals_.append(copy)
    for w in range(4):
        for k in range(1, pair_n):
            arrived(w, k, 0, pair_send, pair_recv).wait_recv()
            pass_on(w, k, 0, in_send, in_recv, a_device)
            pass_on(w, k, 0, out_send, out_recv, b_device)
            to_core(w, k, 0)
    for w in range(4):
        for k in range(1, pair_n):
            arrived(w, k, 1, in_send, in_recv).wait_recv()
            if route[w] == "b":
                pass_on(w, k, 1, diag_send, diag_recv, b_device)
            to_core(w, k, 1)
            arrived(w, k, 2, out_send, out_recv).wait_recv()
            if route[w] == "a":
                pass_on(w, k, 2, diag_send, diag_recv, a_device)
            to_core(w, k, 2)
    for w in range(4):
        for k in range(1, pair_n):
            arrived(w, k, 3, diag_send, diag_recv).wait_recv()
            to_core(w, k, 3)
    for w in range(4):
        place = outs[w].at[pair * 2 + 1 - core]
        remote(place, place, core_send.at[w], core_recv.at[w], core_device).wait_recv()
        for k in range(1, pair_n):
            other = ((pair + pair_n - k) % pair_n) * 2 + 1 - core
            for kind in range(4):
                place = cut(outs[w].at[other], w, pieces[kind])
                remote(
                    place, place, piece_send.at[w, k - 1, kind], piece_recv.at[w, k - 1, kind],
                    core_device,
                ).wait_recv()
    for k in range(len(gain_peers)):
        remote(
            shards[4], outs[4].at[member], gain_send.at[k], gain_recv.at[k], core_device
        ).wait_recv()
    for copy in pending:
        copy.wait_send()
    for copy in locals_:
        copy.wait()


def gather_weights(shards, n_copies, n_group):
    pair_n = n_group // 2
    others = max(pair_n - 1, 1)
    dma = pltpu.SemaphoreType.DMA
    return pl.pallas_call(
        functools.partial(gather_kernel, n_copies, n_group),
        out_shape=[jax.ShapeDtypeStruct((n_group,) + w.shape, w.dtype) for w in shards],
        in_specs=[pl.BlockSpec(memory_space=pltpu.VMEM)] * 5,
        out_specs=[pl.BlockSpec(memory_space=pl.ANY)] * 5,
        scratch_shapes=[
            dma((5,)),
            dma((4,)),
            dma((4,)),
            *[dma((4, others)) for _ in range(8)],
            dma((4, others, 4)),
            dma((4, others, 4)),
            dma((n_group - 1,)),
            dma((n_group - 1,)),
        ],
        compiler_params=pltpu.CompilerParams(
            collective_id=1, has_side_effects=True, vmem_limit_bytes=40 * 1024 * 1024
        ),
    )(*shards)


def per_device(
    inputs,
    cotangent,
    w_query,
    key_weight,
    value_weight,
    w_output,
    w_gate,
    w_up,
    w_down,
    attn_gain,
    mlp_gain,
):
    n_copies = lax.axis_size("dp")
    n_group = lax.axis_size("fsdp")
    width = inputs.shape[-1]
    rows = width // n_group
    attn_shard = jnp.concatenate([w_query, key_weight, w_output, value_weight], axis=1)
    gain_flat = jnp.concatenate([attn_gain, mlp_gain])
    gain_lines = -(-gain_flat.shape[0] // 2048) * 16
    gain_shard = jnp.pad(gain_flat, (0, gain_lines * 128 - gain_flat.shape[0]))
    full_attn, full_gate, full_up, full_down, full_gain = gather_weights(
        (attn_shard, w_gate, w_up, w_down, gain_shard.reshape(gain_lines, 128)),
        n_copies,
        n_group,
    )
    full_attn = full_attn.reshape(width, -1)
    full_gain = full_gain.reshape(n_group, -1)
    cut = [w_query.shape[1], key_weight.shape[1], w_output.shape[1], value_weight.shape[1]]
    edges = [sum(cut[:k]) for k in range(5)]
    gathered = (
        full_attn[:, edges[0] : edges[1]],
        full_attn[:, edges[1] : edges[2]],
        full_attn[:, edges[3] : edges[4]],
        full_attn[:, edges[2] : edges[3]],
        full_gate.reshape(width, -1),
        full_up.reshape(width, -1),
        full_down.reshape(-1, width),
        full_gain[:, :rows].reshape(width),
        full_gain[:, rows : 2 * rows].reshape(width),
    )
    outputs, saved = forward_pass(inputs, gathered)
    grad_inputs, grads = backward_pass(cotangent, gathered, saved)
    scale = float(n_copies * n_group * inputs.shape[0] * inputs.shape[1]) ** (-0.5)
    bf = jnp.bfloat16
    attn_block = jnp.concatenate(
        [g.astype(bf) for g in (grads[0], grads[1], grads[3], grads[2])], axis=1
    )
    gain_block = jnp.concatenate(
        [g.astype(bf).reshape(n_group, rows) for g in (grads[7], grads[8])], axis=1
    )
    big, down_sum, gain_sum = reduce_blocks(
        (attn_block, grads[4].astype(bf), grads[5].astype(bf)),
        grads[6].astype(bf),
        gain_block,
        n_copies,
        n_group,
    )

    def scaled(value):
        return value.astype(jnp.float32) * scale

    return (
        outputs,
        grad_inputs,
        scaled(big[0, :, edges[0] : edges[1]]),
        scaled(big[0, :, edges[1] : edges[2]]),
        scaled(big[0, :, edges[3] : edges[4]]),
        scaled(big[0, :, edges[2] : edges[3]]),
        scaled(big[1]),
        scaled(big[2]),
        scaled(down_sum.T),
        scaled(gain_sum[:rows]),
        scaled(gain_sum[rows:]),
    )


def solution(mesh):
    return jax.shard_map(
        per_device,
        mesh=mesh,
        in_specs=(
            P(("dp", "fsdp"), None, None),
            P(("dp", "fsdp"), None, None),
            P("fsdp", None),
            P("fsdp", None),
            P("fsdp", None),
            P("fsdp", None),
            P("fsdp", None),
            P("fsdp", None),
            P("fsdp", None),
            P("fsdp"),
            P("fsdp"),
        ),
        out_specs=(
            P(("dp", "fsdp"), None, None),
            P(("dp", "fsdp"), None, None),
            P("fsdp", None),
            P("fsdp", None),
            P("fsdp", None),
            P("fsdp", None),
            P("fsdp", None),
            P("fsdp", None),
            P("fsdp", None),
            P("fsdp"),
            P("fsdp"),
        ),
        check_vma=False,
    )
```

```python
import functools

import jax
import jax.numpy as jnp
from jax import lax
from jax.experimental import pallas as pl
from jax.experimental.pallas import tpu as pltpu
from jax.sharding import PartitionSpec as P

QUERY_HEADS = 15
KEY_VALUE_HEADS = 5
HEAD_DIMENSION = 64


EPS = 1e-05
ROPE_BASE = 10000.0


def matrix_product(left_matrix, right_matrix):
    return jnp.dot(left_matrix, right_matrix, preferred_element_type=jnp.float32)


def matmul_tn(left_matrix, right_matrix):
    return lax.dot_general(
        left_matrix, right_matrix, (((0,), (0,)), ((), ())), preferred_element_type=jnp.float32
    )


def matmul_nt(left_matrix, right_matrix):
    return lax.dot_general(
        left_matrix, right_matrix, (((1,), (1,)), ((), ())), preferred_element_type=jnp.float32
    )


def rope_tables(sequence_length, head_size):
    half_size = head_size // 2
    frequency = ROPE_BASE ** (-(jnp.arange(half_size, dtype=jnp.float32) * (2.0 / head_size)))
    angles = jnp.arange(sequence_length, dtype=jnp.float32)[:, None] * frequency[None, :]
    return (jnp.cos(angles), jnp.sin(angles))


def apply_rotary(tensor, cosine_table, sine_lookup, direction):
    half_size = tensor.shape[-1] // 2
    first_half = tensor[..., :half_size]
    second_half = tensor[..., half_size:]
    cos_wide = cosine_table[None, :, None, :]
    sin_wide = sine_lookup[None, :, None, :]
    return jnp.concatenate(
        [
            first_half * cos_wide - direction * second_half * sin_wide,
            second_half * cos_wide + direction * first_half * sin_wide,
        ],
        axis=-1,
    )


def norm_forward(values_in, gain_vec):
    inv_rms = lax.rsqrt(jnp.mean(values_in * values_in, axis=-1, keepdims=True) + EPS)
    unit_rows = values_in * inv_rms
    normed = (unit_rows * gain_vec.astype(jnp.float32)).astype(jnp.bfloat16)
    return (unit_rows, inv_rms, normed)


def norm_backward(grad_out, unit_rows, inv_rms, gain_vec):
    grad_gain = jnp.sum(grad_out * unit_rows, axis=(0, 1))
    grad_unit = grad_out * gain_vec.astype(jnp.float32)
    grad_in = inv_rms * (
        grad_unit - unit_rows * jnp.mean(grad_unit * unit_rows, axis=-1, keepdims=True)
    )
    return (grad_in, grad_gain)


def scores_of(query_rot, key_rot):
    local_sequences, sequence_length, heads_q, head_size = query_rot.shape
    heads_kv = key_rot.shape[2]
    grouped = query_rot.reshape(
        local_sequences, sequence_length, heads_kv, heads_q // heads_kv, head_size
    )
    scores = jnp.einsum(
        "sqhgd,skhd->shgqk", grouped, key_rot, preferred_element_type=jnp.float32
    ) * head_size ** (-0.5)
    positions = jnp.arange(sequence_length)
    allowed = positions[:, None] >= positions[None, :]
    return (grouped, jnp.where(allowed, scores, -1e30))


def attend(query_rot, key_rot, value_low_precision):
    grouped, scores = scores_of(query_rot, key_rot)
    peak_row = jnp.max(scores, axis=-1, keepdims=True)
    logsum = peak_row + jnp.log(jnp.sum(jnp.exp(scores - peak_row), axis=-1, keepdims=True))
    probs_bf = jnp.exp(scores - logsum).astype(jnp.bfloat16)
    attn_mixed = jnp.einsum(
        "shgqk,skhd->sqhgd", probs_bf, value_low_precision, preferred_element_type=jnp.float32
    )
    local_sequences, sequence_length = (query_rot.shape[0], query_rot.shape[1])
    return (attn_mixed.reshape(local_sequences, sequence_length, -1).astype(jnp.bfloat16), logsum)


def attend_back(query_rot, key_rot, value_low_precision, logsum, grad_mixed):
    grouped, scores = scores_of(query_rot, key_rot)
    probs = jnp.exp(scores - logsum)
    probs_bf = probs.astype(jnp.bfloat16)
    grad_grouped = grad_mixed.reshape(grouped.shape)
    value_gradient = jnp.einsum(
        "shgqk,sqhgd->skhd", probs_bf, grad_grouped, preferred_element_type=jnp.float32
    )
    grad_probs = jnp.einsum(
        "sqhgd,skhd->shgqk", grad_grouped, value_low_precision, preferred_element_type=jnp.float32
    )
    row_dot = jnp.sum(probs * grad_probs, axis=-1, keepdims=True)
    grad_scores = (probs * (grad_probs - row_dot) * query_rot.shape[-1] ** (-0.5)).astype(
        jnp.bfloat16
    )
    grad_query = jnp.einsum(
        "shgqk,skhd->sqhgd", grad_scores, key_rot, preferred_element_type=jnp.float32
    )
    key_gradient = jnp.einsum(
        "shgqk,sqhgd->skhd", grad_scores, grouped, preferred_element_type=jnp.float32
    )
    return (grad_query.reshape(query_rot.shape), key_gradient, value_gradient)


def forward_pass(inputs, weights):
    w_query, key_weight, value_weight, w_output, w_gate, w_up, w_down, attn_gain, mlp_gain = weights
    local_sequences, sequence_length, width = inputs.shape
    cosine_table, sine_lookup = rope_tables(sequence_length, HEAD_DIMENSION)
    resid_in = inputs.astype(jnp.float32)
    unit_one, inv_one, normed_one = norm_forward(resid_in, attn_gain)
    flattened_first = normed_one.reshape(-1, width)
    query_proj = matrix_product(flattened_first, w_query).reshape(
        local_sequences, sequence_length, QUERY_HEADS, HEAD_DIMENSION
    )
    projected_key = matrix_product(flattened_first, key_weight).reshape(
        local_sequences, sequence_length, KEY_VALUE_HEADS, HEAD_DIMENSION
    )
    value_low_precision = (
        matrix_product(flattened_first, value_weight)
        .astype(jnp.bfloat16)
        .reshape(local_sequences, sequence_length, KEY_VALUE_HEADS, HEAD_DIMENSION)
    )
    query_rot = apply_rotary(query_proj, cosine_table, sine_lookup, 1.0).astype(jnp.bfloat16)
    key_rot = apply_rotary(projected_key, cosine_table, sine_lookup, 1.0).astype(jnp.bfloat16)
    attn_mixed, logsum = attend(query_rot, key_rot, value_low_precision)
    flat_mixed = attn_mixed.reshape(-1, QUERY_HEADS * HEAD_DIMENSION)
    resid_mid = resid_in + matrix_product(flat_mixed, w_output).reshape(inputs.shape)
    unit_two, inv_two, normed_two = norm_forward(resid_mid, mlp_gain)
    flat_two = normed_two.reshape(-1, width)
    gate_pre = matrix_product(flat_two, w_gate)
    up_proj = matrix_product(flat_two, w_up)
    sigmoid_gate = jax.nn.sigmoid(gate_pre)
    hidden = (gate_pre * sigmoid_gate * up_proj).astype(jnp.bfloat16)
    outputs = (resid_mid + matrix_product(hidden, w_down).reshape(inputs.shape)).astype(
        jnp.bfloat16
    )
    saved = (
        unit_one,
        inv_one,
        flattened_first,
        query_rot,
        key_rot,
        value_low_precision,
        flat_mixed,
        logsum,
        unit_two,
        inv_two,
        flat_two,
        gate_pre,
        up_proj,
        sigmoid_gate,
        hidden,
    )
    return (outputs, saved)


def backward_pass(cotangent, weights, saved):
    w_query, key_weight, value_weight, w_output, w_gate, w_up, w_down, attn_gain, mlp_gain = weights
    (
        unit_one,
        inv_one,
        flattened_first,
        query_rot,
        key_rot,
        value_low_precision,
        flat_mixed,
        logsum,
        unit_two,
        inv_two,
        flat_two,
        gate_pre,
        up_proj,
        sigmoid_gate,
        hidden,
    ) = saved
    local_sequences, sequence_length, width = cotangent.shape
    cosine_table, sine_lookup = rope_tables(sequence_length, HEAD_DIMENSION)
    cot_flat = cotangent.reshape(-1, width)
    sum_down = matmul_tn(cot_flat, hidden)
    grad_hidden = matmul_nt(cot_flat, w_down)
    grad_gate_bf = (
        grad_hidden * up_proj * sigmoid_gate * (1.0 + gate_pre * (1.0 - sigmoid_gate))
    ).astype(jnp.bfloat16)
    grad_up_bf = (grad_hidden * gate_pre * sigmoid_gate).astype(jnp.bfloat16)
    sum_gate = matmul_tn(flat_two, grad_gate_bf)
    sum_up = matmul_tn(flat_two, grad_up_bf)
    grad_normed_two = matmul_nt(grad_gate_bf, w_gate) + matmul_nt(grad_up_bf, w_up)
    grad_norm_two, sum_mlp_gain = norm_backward(
        grad_normed_two.reshape(cotangent.shape), unit_two, inv_two, mlp_gain
    )
    grad_resid_mid = cotangent.astype(jnp.float32) + grad_norm_two
    grad_mid_bf = grad_resid_mid.astype(jnp.bfloat16).reshape(-1, width)
    grad_mixed_bf = (
        matmul_nt(grad_mid_bf, w_output)
        .astype(jnp.bfloat16)
        .reshape(local_sequences, sequence_length, QUERY_HEADS, HEAD_DIMENSION)
    )
    grad_query, key_gradient, value_gradient = attend_back(
        query_rot, key_rot, value_low_precision, logsum, grad_mixed_bf
    )
    grad_query_bf = (
        apply_rotary(grad_query, cosine_table, sine_lookup, -1.0)
        .astype(jnp.bfloat16)
        .reshape(-1, QUERY_HEADS * HEAD_DIMENSION)
    )
    key_gradient_low = (
        apply_rotary(key_gradient, cosine_table, sine_lookup, -1.0)
        .astype(jnp.bfloat16)
        .reshape(-1, KEY_VALUE_HEADS * HEAD_DIMENSION)
    )
    value_gradient_low = value_gradient.astype(jnp.bfloat16).reshape(
        -1, KEY_VALUE_HEADS * HEAD_DIMENSION
    )
    kv_width = key_gradient_low.shape[1]
    sum_attn = matmul_tn(
        jnp.concatenate([flattened_first, flat_mixed], axis=0),
        jnp.concatenate(
            [
                jnp.concatenate(
                    [
                        grad_query_bf,
                        key_gradient_low,
                        jnp.zeros_like(grad_mid_bf),
                        value_gradient_low,
                    ],
                    axis=1,
                ),
                jnp.pad(
                    grad_mid_bf,
                    ((0, 0), (grad_query_bf.shape[1] + kv_width, kv_width)),
                ),
            ],
            axis=0,
        ),
    )
    grad_normed_one = (
        matmul_nt(grad_query_bf, w_query)
        + matmul_nt(key_gradient_low, key_weight)
        + matmul_nt(value_gradient_low, value_weight)
    )
    grad_norm_one, sum_attn_gain = norm_backward(
        grad_normed_one.reshape(cotangent.shape), unit_one, inv_one, attn_gain
    )
    grad_inputs = grad_resid_mid + grad_norm_one
    return (
        grad_inputs,
        (
            sum_attn,
            sum_gate,
            sum_up,
            sum_down,
            sum_attn_gain,
            sum_mlp_gain,
        ),
    )


CHUNK = 512


def dp_split(n_copies):
    outer = 4 if n_copies % 4 == 0 else 1
    return n_copies // outer, outer


def reduce_kernel(n_copies, n_group, per_block, down_direct, *refs):
    sources = refs[:5]
    out_hbm, out_down, out_gain = refs[5:8]
    own, from_core, from_pair, from_inner, from_outer, final = refs[8:14]
    (load_sem, store_sem, send_core, recv_core, send_pair, recv_pair, send_in, recv_in,
     send_out, recv_out, send_ago, recv_ago, send_agi, recv_agi) = refs[14:]
    inner_n, outer_n = dp_split(n_copies)
    pair_n = n_group // 2
    steps = 4 * per_block + 1
    down_start = 3 * per_block
    copy_id = lax.axis_index("dp")
    member = lax.axis_index("fsdp")
    pair, core = member // 2, member % 2
    outer, inner = copy_id // inner_n, copy_id % inner_n
    piece = CHUNK // outer_n

    def pair_peer(k):
        return (pair + k) % pair_n

    def inner_peer(k):
        return (inner + k) % inner_n

    def outer_peer(k):
        return (outer + k) % outer_n

    def columns(z):
        return pl.ds(pl.multiple_of(z * piece, piece), piece)

    core_device = (copy_id, pair * 2 + (1 - core))
    barrier = pltpu.get_barrier_semaphore()
    devices = [core_device]
    devices += [(copy_id, pair_peer(k) * 2 + core) for k in range(1, pair_n)]
    devices += [(outer * inner_n + inner_peer(k), member) for k in range(1, inner_n)]
    devices += [(outer_peer(k) * inner_n + inner, member) for k in range(1, outer_n)]
    for device in devices:
        pl.semaphore_signal(
            barrier, inc=1, device_id=device, device_id_type=pl.DeviceIdType.MESH
        )
    pl.semaphore_wait(barrier, len(devices))

    def remote(src, dst, send, recv, device):
        return pltpu.make_async_remote_copy(
            src_ref=src,
            dst_ref=dst,
            send_sem=send,
            recv_sem=recv,
            device_id=device,
            device_id_type=pl.DeviceIdType.MESH,
        )

    def core_copy(t, source, c):
        cols = pl.ds(c * CHUNK, CHUNK)
        return remote(
            source.at[:, 1 - core, :, :, cols],
            from_core.at[t],
            send_core.at[t],
            recv_core.at[t],
            core_device,
        )

    def load_copy(t, source, c):
        cols = pl.ds(c * CHUNK, CHUNK)
        return pltpu.make_async_copy(
            source.at[:, core, :, :, cols], own.at[t], load_sem.at[t]
        )

    def pair_copy(t, k):
        return remote(
            own.at[t, pair_peer(k)],
            from_pair.at[t, k - 1],
            send_pair.at[t, k - 1],
            recv_pair.at[t, k - 1],
            (copy_id, pair_peer(k) * 2 + core),
        )

    def inner_copy(t, k):
        return remote(
            own.at[t, pair, inner_peer(k)],
            from_inner.at[t, k - 1],
            send_in.at[t, k - 1],
            recv_in.at[t, k - 1],
            (outer * inner_n + inner_peer(k), member),
        )

    def outer_copy(t, k):
        return remote(
            own.at[t, pair, inner, :, columns(outer_peer(k))],
            from_outer.at[t, k - 1],
            send_out.at[t, k - 1],
            recv_out.at[t, k - 1],
            (outer_peer(k) * inner_n + inner, member),
        )

    def spread_outer(t, k):
        place = final.at[t, inner, :, columns(outer)]
        return remote(
            place,
            place,
            send_ago.at[t, k - 1],
            recv_ago.at[t, k - 1],
            (outer_peer(k) * inner_n + inner, member),
        )

    def landed_outer(t, k):
        place = final.at[t, inner, :, columns((outer + outer_n - k) % outer_n)]
        return remote(
            place,
            place,
            send_ago.at[t, k - 1],
            recv_ago.at[t, k - 1],
            (outer_peer(k) * inner_n + inner, member),
        )

    def spread_inner(t, k):
        place = final.at[t, inner]
        return remote(
            place,
            place,
            send_agi.at[t, k - 1],
            recv_agi.at[t, k - 1],
            (outer * inner_n + inner_peer(k), member),
        )

    def landed_inner(t, k):
        place = final.at[t, (inner + inner_n - k) % inner_n]
        return remote(
            place,
            place,
            send_agi.at[t, k - 1],
            recv_agi.at[t, k - 1],
            (outer * inner_n + inner_peer(k), member),
        )

    def store_copy(t, target):
        return pltpu.make_async_copy(final.at[t], target, store_sem.at[t])

    def start_store(t):
        @pl.when(t < down_start)
        def _():
            cols = pl.ds(pl.multiple_of(lax.rem(t, per_block) * CHUNK, CHUNK), CHUNK)
            store_copy(t, out_hbm.at[t // per_block, :, :, cols]).start()

        @pl.when((t >= down_start) & (t < steps - 1))
        def _():
            c = t - down_start
            if down_direct:
                cols = pl.ds(pl.multiple_of(c * tile, tile), tile)
                for b in range(n_group):
                    pltpu.make_async_copy(
                        final.at[t, :, :, pl.ds(b * tile, tile)],
                        out_down.at[b, :, :, cols],
                        store_sem.at[t],
                    ).start()
            else:
                cols = pl.ds(pl.multiple_of(c * CHUNK, CHUNK), CHUNK)
                store_copy(t, out_down.at[:, :, cols]).start()

        @pl.when(t == steps - 1)
        def _():
            store_copy(t, out_gain).start()

    tile = CHUNK // n_group
    part_width = sources[3].shape[-1] // n_group
    for t in range(steps):
        block, c = t // per_block, t % per_block
        if block == 3 and down_direct:
            for p in range(pair_n):
                for b in range(n_group):
                    place = (slice(None), slice(None), pl.ds(b * tile, tile))
                    theirs = pl.multiple_of((p * 2 + 1 - core) * part_width + c * tile, tile)
                    mine = pl.multiple_of((p * 2 + core) * part_width + c * tile, tile)
                    remote(
                        sources[3].at[b, :, :, pl.ds(theirs, tile)],
                        from_core.at[(t, p) + place],
                        send_core.at[t],
                        recv_core.at[t],
                        core_device,
                    ).start()
                    pltpu.make_async_copy(
                        sources[3].at[b, :, :, pl.ds(mine, tile)],
                        own.at[(t, p) + place],
                        load_sem.at[t],
                    ).start()
        else:
            core_copy(t, sources[block], c).start()
            load_copy(t, sources[block], c).start()

    def stage_core(t):
        core_copy(t, sources[0], 0).wait_recv()
        load_copy(t, sources[0], 0).wait()

        def add(i, carry):
            p, x = i // inner_n, i % inner_n
            total = own[t, p, x].astype(jnp.float32) + from_core[t, p, x].astype(jnp.float32)
            own[t, p, x] = total.astype(own.dtype)
            return carry

        lax.fori_loop(0, pair_n * inner_n, add, 0)
        for k in range(1, pair_n):
            pair_copy(t, k).start()

    def stage_pair(t):
        for k in range(1, pair_n):
            pair_copy(t, k).wait_recv()

        def add(x, carry):
            total = own[t, pair, x].astype(jnp.float32)
            for k in range(1, pair_n):
                total += from_pair[t, k - 1, x].astype(jnp.float32)
            own[t, pair, x] = total.astype(own.dtype)
            return carry

        lax.fori_loop(0, inner_n, add, 0)
        for k in range(1, inner_n):
            inner_copy(t, k).start()

    def stage_inner(t):
        total = own[t, pair, inner].astype(jnp.float32)
        for k in range(1, inner_n):
            inner_copy(t, k).wait_recv()
            total += from_inner[t, k - 1].astype(jnp.float32)
        own[t, pair, inner] = total.astype(own.dtype)
        for k in range(1, outer_n):
            outer_copy(t, k).start()

    def stage_outer(t):
        total = own[t, pair, inner, :, columns(outer)].astype(jnp.float32)
        for k in range(1, outer_n):
            outer_copy(t, k).wait_recv()
            total += from_outer[t, k - 1].astype(jnp.float32)
        final[t, inner, :, columns(outer)] = total.astype(final.dtype)
        for k in range(1, outer_n):
            spread_outer(t, k).start()

    def stage_spread(t):
        for k in range(1, outer_n):
            landed_outer(t, k).wait_recv()
        for k in range(1, inner_n):
            spread_inner(t, k).start()

    def stage_store(t):
        for k in range(1, inner_n):
            landed_inner(t, k).wait_recv()
        start_store(t)

    lags = ((stage_core, 0), (stage_pair, 3), (stage_inner, 4), (stage_outer, 5),
            (stage_spread, 6), (stage_store, 7))

    def step(s, carry):
        for stage, lag in lags:
            @pl.when((s >= lag) & (s < steps + lag))
            def _():
                stage(s - lag)
        return carry

    lax.fori_loop(0, steps + 7, step, 0)

    def drain(t, carry):
        core_copy(t, sources[0], 0).wait_send()
        for k in range(1, pair_n):
            pair_copy(t, k).wait_send()
        for k in range(1, inner_n):
            inner_copy(t, k).wait_send()
            spread_inner(t, k).wait_send()
        for k in range(1, outer_n):
            outer_copy(t, k).wait_send()
            spread_outer(t, k).wait_send()
        store_copy(t, out_gain).wait()
        return carry

    lax.fori_loop(0, steps, drain, 0)


def reduce_blocks(blocks, down, gains, n_copies, n_group):
    total_rows, total_columns = blocks[0].shape
    inner_n, outer_n = dp_split(n_copies)
    pair_n = n_group // 2
    part = total_rows // (n_group * inner_n)
    per_block = total_columns // CHUNK
    steps = 4 * per_block + 1
    part_width = total_columns // n_group
    down_direct = n_group * 128 == CHUNK and part_width % 128 == 0
    piece = CHUNK // outer_n
    bf = jnp.bfloat16
    dma = pltpu.SemaphoreType.DMA

    def many(n):
        return dma((steps, max(n - 1, 1)))

    grouped = (pair_n, 2, inner_n, part)
    if down_direct:
        down = down.reshape(n_group, inner_n, part, total_columns)
        down_shape = (n_group, inner_n, part, part_width)
    else:
        down = (
            down.reshape(n_group, total_rows // n_group, n_group, part_width)
            .transpose(2, 1, 0, 3)
            .reshape(*grouped, total_columns)
        )
        down_shape = (inner_n, part, total_columns)
    gain_width = gains.shape[-1]
    gains = (
        jnp.pad(gains, ((0, 0), (0, inner_n * part * CHUNK - gain_width)))
        .reshape(*grouped, CHUNK)
    )
    big, down_sum, gain_sum = pl.pallas_call(
        functools.partial(reduce_kernel, n_copies, n_group, per_block, down_direct),
        out_shape=[
            jax.ShapeDtypeStruct((3, inner_n, part, total_columns), bf),
            jax.ShapeDtypeStruct(down_shape, bf),
            jax.ShapeDtypeStruct((inner_n, part, CHUNK), bf),
        ],
        in_specs=[pl.BlockSpec(memory_space=pl.ANY)] * 5,
        out_specs=[pl.BlockSpec(memory_space=pl.ANY)] * 3,
        scratch_shapes=[
            pltpu.VMEM((steps, pair_n, inner_n, part, CHUNK), bf),
            pltpu.VMEM((steps, pair_n, inner_n, part, CHUNK), bf),
            pltpu.VMEM((steps, max(pair_n - 1, 1), inner_n, part, CHUNK), bf),
            pltpu.VMEM((steps, max(inner_n - 1, 1), part, CHUNK), bf),
            pltpu.VMEM((steps, max(outer_n - 1, 1), part, piece), bf),
            pltpu.VMEM((steps, inner_n, part, CHUNK), bf),
            dma((steps,)),
            dma((steps,)),
            dma((steps,)),
            dma((steps,)),
            many(pair_n),
            many(pair_n),
            many(inner_n),
            many(inner_n),
            many(outer_n),
            many(outer_n),
            many(outer_n),
            many(outer_n),
            many(inner_n),
            many(inner_n),
        ],
        compiler_params=pltpu.CompilerParams(
            collective_id=0, has_side_effects=True, vmem_limit_bytes=60 * 1024 * 1024
        ),
    )(*(b.reshape(*grouped, total_columns) for b in blocks), down, gains)
    rows = inner_n * part
    big = big.reshape(3, rows, total_columns)
    if down_direct:
        down_sum = down_sum.reshape(total_rows, part_width)
    else:
        down_sum = (
            down_sum.reshape(rows, n_group, part_width).transpose(1, 0, 2).reshape(total_rows, part_width)
        )
    return big, down_sum, gain_sum.reshape(-1)[:gain_width]


def gather_kernel(n_copies, n_group, *refs):
    shards = refs[:5]
    outs = refs[5:10]
    (own_sem, core_send, core_recv, pair_send, pair_recv, in_send, in_recv, out_send, out_recv,
     diag_send, diag_recv, piece_send, piece_recv, gain_send, gain_recv) = refs[10:]
    inner_n, outer_n = dp_split(n_copies)
    pair_n = n_group // 2
    copy_id = lax.axis_index("dp")
    member = lax.axis_index("fsdp")
    pair, core = member // 2, member % 2
    outer, inner = copy_id // inner_n, copy_id % inner_n
    a_bit, b_bit = inner % 2, outer % 2
    a_device = (outer * inner_n + inner + 1 - 2 * a_bit, member)
    b_device = ((outer + 1 - 2 * b_bit) * inner_n + inner, member)
    core_device = (copy_id, pair * 2 + 1 - core)

    def peer(k):
        return (copy_id, ((pair + k) % pair_n) * 2 + core)

    devices = [core_device, a_device, b_device]
    devices += [peer(k) for k in range(1, pair_n)]
    devices += [(copy_id, ((pair + k) % pair_n) * 2 + 1 - core) for k in range(1, pair_n)]
    barrier = pltpu.get_barrier_semaphore()
    for device in devices:
        pl.semaphore_signal(
            barrier, inc=1, device_id=device, device_id_type=pl.DeviceIdType.MESH
        )
    pl.semaphore_wait(barrier, len(devices))

    def remote(src, dst, send, recv, device):
        return pltpu.make_async_remote_copy(
            src_ref=src,
            dst_ref=dst,
            send_sem=send,
            recv_sem=recv,
            device_id=device,
            device_id_type=pl.DeviceIdType.MESH,
        )

    def cut(ref, w, q):
        rows, columns = shards[w].shape
        if w < 3:
            size = columns // 4
            return ref.at[:, pl.ds(pl.multiple_of(q * size, size), size)]
        size = rows // 4
        return ref.at[pl.ds(pl.multiple_of(q * size, size), size), :]

    def index(a, b):
        return a * 2 + b

    pieces = (
        index(a_bit, b_bit),
        index(1 - a_bit, b_bit),
        index(a_bit, 1 - b_bit),
        index(1 - a_bit, 1 - b_bit),
    )
    route = ("a", "b", "y", "y")
    pending = []

    def launch(copy):
        copy.start()
        pending.append(copy)

    def source(k):
        return ((pair + pair_n - k) % pair_n) * 2 + core

    def arrived(w, k, kind, send, recv):
        place = cut(outs[w].at[source(k)], w, pieces[kind])
        return remote(place, place, send.at[w, k - 1], recv.at[w, k - 1], core_device)

    def pass_on(w, k, kind, send, recv, device):
        place = cut(outs[w].at[source(k)], w, pieces[kind])
        launch(remote(place, place, send.at[w, k - 1], recv.at[w, k - 1], device))

    def to_core(w, k, kind):
        place = cut(outs[w].at[source(k)], w, pieces[kind])
        launch(
            remote(
                place, place, piece_send.at[w, k - 1, kind], piece_recv.at[w, k - 1, kind],
                core_device,
            )
        )

    gain_peers = [core_device]
    gain_peers += [(copy_id, ((pair + k) % pair_n) * 2 + core) for k in range(1, pair_n)]
    gain_peers += [(copy_id, ((pair + k) % pair_n) * 2 + 1 - core) for k in range(1, pair_n)]
    for k, device in enumerate(gain_peers):
        launch(remote(shards[4], outs[4].at[member], gain_send.at[k], gain_recv.at[k], device))
    for w in range(4):
        for k in range(1, pair_n):
            launch(
                remote(
                    cut(shards[w], w, pieces[0]),
                    cut(outs[w].at[member], w, pieces[0]),
                    pair_send.at[w, k - 1],
                    pair_recv.at[w, k - 1],
                    peer(k),
                )
            )
    for w in range(4):
        if route[w] == "y":
            for k in range(1, pair_n):
                launch(
                    remote(
                        cut(shards[w], w, pieces[3]),
                        cut(outs[w].at[member], w, pieces[3]),
                        diag_send.at[w, k - 1],
                        diag_recv.at[w, k - 1],
                        peer(k),
                    )
                )
    locals_ = []
    for w in range(4):
        launch(remote(shards[w], outs[w].at[member], core_send.at[w], core_recv.at[w], core_device))
    for w in range(5):
        copy = pltpu.make_async_copy(shards[w], outs[w].at[member], own_sem.at[w])
        copy.start()
        locals_.append(copy)
    for w in range(4):
        for k in range(1, pair_n):
            arrived(w, k, 0, pair_send, pair_recv).wait_recv()
            pass_on(w, k, 0, in_send, in_recv, a_device)
            pass_on(w, k, 0, out_send, out_recv, b_device)
            to_core(w, k, 0)
    for w in range(4):
        for k in range(1, pair_n):
            arrived(w, k, 1, in_send, in_recv).wait_recv()
            if route[w] == "b":
                pass_on(w, k, 1, diag_send, diag_recv, b_device)
            to_core(w, k, 1)
            arrived(w, k, 2, out_send, out_recv).wait_recv()
            if route[w] == "a":
                pass_on(w, k, 2, diag_send, diag_recv, a_device)
            to_core(w, k, 2)
    for w in range(4):
        for k in range(1, pair_n):
            arrived(w, k, 3, diag_send, diag_recv).wait_recv()
            to_core(w, k, 3)
    for w in range(4):
        place = outs[w].at[pair * 2 + 1 - core]
        remote(place, place, core_send.at[w], core_recv.at[w], core_device).wait_recv()
        for k in range(1, pair_n):
            other = ((pair + pair_n - k) % pair_n) * 2 + 1 - core
            for kind in range(4):
                place = cut(outs[w].at[other], w, pieces[kind])
                remote(
                    place, place, piece_send.at[w, k - 1, kind], piece_recv.at[w, k - 1, kind],
                    core_device,
                ).wait_recv()
    for k in range(len(gain_peers)):
        remote(
            shards[4], outs[4].at[member], gain_send.at[k], gain_recv.at[k], core_device
        ).wait_recv()
    for copy in pending:
        copy.wait_send()
    for copy in locals_:
        copy.wait()


def gather_weights(shards, n_copies, n_group):
    pair_n = n_group // 2
    others = max(pair_n - 1, 1)
    dma = pltpu.SemaphoreType.DMA
    return pl.pallas_call(
        functools.partial(gather_kernel, n_copies, n_group),
        out_shape=[jax.ShapeDtypeStruct((n_group,) + w.shape, w.dtype) for w in shards],
        in_specs=[pl.BlockSpec(memory_space=pltpu.VMEM)] * 5,
        out_specs=[pl.BlockSpec(memory_space=pl.ANY)] * 5,
        scratch_shapes=[
            dma((5,)),
            dma((4,)),
            dma((4,)),
            *[dma((4, others)) for _ in range(8)],
            dma((4, others, 4)),
            dma((4, others, 4)),
            dma((n_group - 1,)),
            dma((n_group - 1,)),
        ],
        compiler_params=pltpu.CompilerParams(
            collective_id=1, has_side_effects=True, vmem_limit_bytes=40 * 1024 * 1024
        ),
    )(*shards)


def per_device(
    inputs,
    cotangent,
    w_query,
    key_weight,
    value_weight,
    w_output,
    w_gate,
    w_up,
    w_down,
    attn_gain,
    mlp_gain,
):
    n_copies = lax.axis_size("dp")
    n_group = lax.axis_size("fsdp")
    width = inputs.shape[-1]
    rows = width // n_group
    attn_shard = jnp.concatenate([w_query, key_weight, w_output, value_weight], axis=1)
    gain_flat = jnp.concatenate([attn_gain, mlp_gain])
    gain_lines = -(-gain_flat.shape[0] // 2048) * 16
    gain_shard = jnp.pad(gain_flat, (0, gain_lines * 128 - gain_flat.shape[0]))
    full_attn, full_gate, full_up, full_down, full_gain = gather_weights(
        (attn_shard, w_gate, w_up, w_down, gain_shard.reshape(gain_lines, 128)),
        n_copies,
        n_group,
    )
    full_attn = full_attn.reshape(width, -1)
    full_gain = full_gain.reshape(n_group, -1)
    cut = [w_query.shape[1], key_weight.shape[1], w_output.shape[1], value_weight.shape[1]]
    edges = [sum(cut[:k]) for k in range(5)]
    gathered = (
        full_attn[:, edges[0] : edges[1]],
        full_attn[:, edges[1] : edges[2]],
        full_attn[:, edges[3] : edges[4]],
        full_attn[:, edges[2] : edges[3]],
        full_gate.reshape(width, -1),
        full_up.reshape(width, -1),
        full_down.reshape(-1, width),
        full_gain[:, :rows].reshape(width),
        full_gain[:, rows : 2 * rows].reshape(width),
    )
    outputs, saved = forward_pass(inputs, gathered)
    grad_inputs, grads = backward_pass(cotangent, gathered, saved)
    scale = float(n_copies * n_group * inputs.shape[0] * inputs.shape[1]) ** (-0.5)
    bf = jnp.bfloat16
    gain_block = jnp.concatenate(
        [g.astype(bf).reshape(n_group, rows) for g in (grads[4], grads[5])], axis=1
    )
    big, down_sum, gain_sum = reduce_blocks(
        (grads[0].astype(bf), grads[1].astype(bf), grads[2].astype(bf)),
        grads[3].astype(bf),
        gain_block,
        n_copies,
        n_group,
    )

    def scaled(value):
        return value.astype(jnp.float32) * scale

    return (
        outputs,
        grad_inputs,
        scaled(big[0, :, edges[0] : edges[1]]),
        scaled(big[0, :, edges[1] : edges[2]]),
        scaled(big[0, :, edges[3] : edges[4]]),
        scaled(big[0, :, edges[2] : edges[3]]),
        scaled(big[1]),
        scaled(big[2]),
        scaled(down_sum.T),
        scaled(gain_sum[:rows]),
        scaled(gain_sum[rows:]),
    )


def solution(mesh):
    return jax.shard_map(
        per_device,
        mesh=mesh,
        in_specs=(
            P(("dp", "fsdp"), None, None),
            P(("dp", "fsdp"), None, None),
            P("fsdp", None),
            P("fsdp", None),
            P("fsdp", None),
            P("fsdp", None),
            P("fsdp", None),
            P("fsdp", None),
            P("fsdp", None),
            P("fsdp"),
            P("fsdp"),
        ),
        out_specs=(
            P(("dp", "fsdp"), None, None),
            P(("dp", "fsdp"), None, None),
            P("fsdp", None),
            P("fsdp", None),
            P("fsdp", None),
            P("fsdp", None),
            P("fsdp", None),
            P("fsdp", None),
            P("fsdp", None),
            P("fsdp"),
            P("fsdp"),
        ),
        check_vma=False,
    )
```
